32 devices in a mesh: slide: 2 (over x), row: 16 (over z, y, core).
Axes of the slice: x: 2, y: 2, z: 4, core: 2. Of those that a mesh axis runs over, the one named last changes fastest.
Arguments:
- tokens: bfloat16 [128, 128, 768], P(('slide', 'row')), parts along dimension 0, may hold values from -6 to 6
- norm_gain: float32 [768], replicated, may hold values from 0.1 to 1.9
- query_weight: bfloat16 [768, 768], replicated, may hold values from -0.875 to 0.875
- key_weight: bfloat16 [768, 768], replicated, may hold values from -0.875 to 0.875
- value_weight: bfloat16 [768, 768], replicated, may hold values from -0.21875 to 0.21875
- out_weight: bfloat16 [768, 768], replicated, may hold values from -0.21875 to 0.21875
- head_scale: float32 [12], replicated, may hold values from 0.02 to 0.5
- pool_queries: bfloat16 [16, 768], replicated, may hold values from -24 to 24
Outputs:
- mixed: bfloat16 [128, 128, 768], P(('slide', 'row')), parts along dimension 0
- pooled: float32 [32, 768], P('slide'), parts along dimension 0
The draws below stay inside these ranges and needn't reach their ends.
There are 2 independent parts, one for each index of `slide`. The reference program is written for one: setup_inputs(seed, part) draws one part's arguments, and reference() takes and returns one part's arrays. A program takes and returns all parts, laid end to end along the dimension named above; an argument that names none is the same for every part. Nothing has to cross between parts.
All inputs are finite; a program needn't handle non-finite values.
Results may differ from the reference program's by a relative error of at most 0.007.
The reference program's roundings to bfloat16 on the way count: a program that leaves them out, or rounds other values in their place, can miss the bound.
Values may be sent and summed in bfloat16 or wider, within the bound.
No kernel may reach another device: no remote copies, remote signals or barrier semaphores. Data moves between devices by JAX's collectives and lax.ppermute only.
A program may use at most 128 MiB of HBM per device.

```python
import math
import jax
import jax.numpy as jnp
from jax import lax

HEADS = 12
D = 768
RAD = 4
PQ = 16
ROWS_DEV = 4
COLS = 128
SLAB_ROWS = 64


def block_levels(stream_key, dims, shards, low, high):
    gain, own = 1.0, jax.random.fold_in(stream_key, 6)
    for position, parts in shards:
        heights = jnp.exp(jax.random.uniform(jax.random.fold_in(own, position), (parts,), jnp.float32, low / len(shards), high / len(shards)))
        gain = gain * jnp.repeat(heights, dims[position] // parts).reshape([-1 if axis == position else 1 for axis in range(len(dims))])
    return gain


def centred(rng, shape, scale, limit, shards=(), held_as=jnp.bfloat16):
    result = scale * jax.random.normal(rng, shape, jnp.float32)
    if shards:
        result = result * block_levels(rng, shape, shards, -0.22, 0.18)
    return jnp.clip(result, -limit, limit).astype(held_as)


def setup_inputs(seed: int = 0, part: int = 0) -> dict:
    key_of = jax.random.split(jax.random.key(seed), 9)
    part_keys = jax.random.split(jax.random.fold_in(key_of[8], part), 9)
    return {
        "tokens": centred(part_keys[0], (SLAB_ROWS, COLS, D), 1.0, 6.0, ((0, 16),)),
        "norm_gain": jnp.clip(1.0 + 0.18 * jax.random.normal(key_of[1], (D,), jnp.float32), 0.1, 1.9),
        "query_weight": centred(key_of[2], (D, D), (D // 16) ** -0.5, 0.875),
        "key_weight": centred(key_of[3], (D, D), (D // 16) ** -0.5, 0.875),
        "value_weight": centred(key_of[4], (D, D), D ** -0.5, 0.21875),
        "out_weight": centred(key_of[5], (D, D), D ** -0.5, 0.21875),
        "head_scale": jnp.clip(jnp.exp(jax.random.uniform(key_of[6], (HEADS,), jnp.float32, math.log(0.02), math.log(0.5))), 0.02, 0.5),
        "pool_queries": centred(key_of[7], (PQ, D), 4.0, 24.0),
    }


norm_eps = 1e-06

def normalize(tokens, norm_gain):
    feats = tokens.astype(jnp.float32)
    mean_sq = lax.optimization_barrier(jnp.mean(feats * feats, axis=-1, keepdims=True))
    return (feats * lax.rsqrt(mean_sq + norm_eps) * norm_gain).astype(jnp.bfloat16)

def project(weight, normed, head_count):
    row_count, col_count, feature_width = normed.shape
    flattened = normed.reshape(row_count * col_count, feature_width)
    projected = lax.dot_general(weight, flattened, (((0,), (1,)), ((), ())), preferred_element_type=jnp.float32)
    return projected.astype(jnp.bfloat16).reshape(head_count, feature_width // head_count, row_count, col_count)

def lorentz_time(spatial):
    spatial_f = spatial.astype(jnp.float32)
    return jnp.sqrt(1.0 + lax.optimization_barrier(jnp.sum(spatial_f * spatial_f, axis=1)))

def split_cols(array, group, block, reach):
    blocks = group // block
    lead = array.shape[:-1]
    main_part = array[..., :group].reshape(lead + (blocks, block))
    extra = array[..., block:]
    pad_width = [(0, 0)] * len(lead) + [(0, blocks * block - extra.shape[-1])]
    extra = jnp.pad(extra, pad_width).reshape(lead + (blocks, block))[..., :2 * reach]
    return jnp.concatenate([main_part, extra], axis=-1)

def window_attend(query_heads, key_rows, value_rows, row_inside, head_scale):
    head_count, head_width, row_count, col_count = query_heads.shape
    group = 128 if col_count % 128 == 0 else col_count
    block = 32 if group % 32 == 0 else 16
    blocks = group // block
    tile_rows = 4
    key_tile_rows = tile_rows + 2 * RAD
    key_tile_cols = block + 2 * RAD
    key_pad = jnp.pad(key_rows, ((0, 0), (0, 0), (0, 0), (RAD, RAD)))
    value_pad = jnp.pad(value_rows, ((0, 0), (0, 0), (0, 0), (RAD, RAD)))
    key_time = lorentz_time(key_pad)
    value_time = lorentz_time(value_pad)
    query_time = lorentz_time(query_heads)
    col_global = jnp.arange(col_count + 2 * RAD, dtype=jnp.int32) - RAD
    col_inside = (col_global >= 0) & (col_global < col_count)
    query_row = jnp.arange(tile_rows, dtype=jnp.int32)[:, None, None, None]
    query_col = jnp.arange(block, dtype=jnp.int32)[None, :, None, None]
    key_row = jnp.arange(key_tile_rows, dtype=jnp.int32)[None, None, :, None]
    key_col = jnp.arange(key_tile_cols, dtype=jnp.int32)[None, None, None, :]
    row_gap = key_row - query_row
    col_gap = key_col - query_col
    window_mask = (row_gap >= 0) & (row_gap <= 2 * RAD) & (col_gap >= 0) & (col_gap <= 2 * RAD)
    window_mask = window_mask.reshape(tile_rows * block, key_tile_rows * key_tile_cols)
    col_groups = col_count // group
    tile_count = row_count // tile_rows * col_groups

    def one_tile(tile_index):
        row_start = (tile_index // col_groups * tile_rows).astype(jnp.int32)
        col_start = (tile_index % col_groups * group).astype(jnp.int32)
        zero = jnp.zeros((), jnp.int32)
        query_tile = lax.dynamic_slice(query_heads, (zero, zero, row_start, col_start), (head_count, head_width, tile_rows, group))
        key_tile = lax.dynamic_slice(key_pad, (zero, zero, row_start, col_start), (head_count, head_width, key_tile_rows, group + 2 * RAD))
        value_tile = lax.dynamic_slice(value_pad, (zero, zero, row_start, col_start), (head_count, head_width, key_tile_rows, group + 2 * RAD))
        qtime_tile = lax.dynamic_slice(query_time, (zero, row_start, col_start), (head_count, tile_rows, group))
        ktime_tile = lax.dynamic_slice(key_time, (zero, row_start, col_start), (head_count, key_tile_rows, group + 2 * RAD))
        vtime_tile = lax.dynamic_slice(value_time, (zero, row_start, col_start), (head_count, key_tile_rows, group + 2 * RAD))
        rin_tile = lax.dynamic_slice_in_dim(row_inside, row_start, key_tile_rows, 0)
        cin_tile = lax.dynamic_slice_in_dim(col_inside, col_start, group + 2 * RAD, 0)
        query_blocks = query_tile.reshape(head_count, head_width, tile_rows, blocks, block)
        query_blocks = query_blocks.transpose(0, 3, 1, 2, 4).reshape(head_count, blocks, head_width, tile_rows * block)
        key_blocks = split_cols(key_tile, group, block, RAD).transpose(0, 3, 1, 2, 4)
        key_blocks = key_blocks.reshape(head_count, blocks, head_width, key_tile_rows * key_tile_cols)
        value_blocks = split_cols(value_tile, group, block, RAD).transpose(0, 3, 1, 2, 4)
        value_blocks = value_blocks.reshape(head_count, blocks, head_width, key_tile_rows * key_tile_cols)
        qtime_blocks = qtime_tile.reshape(head_count, tile_rows, blocks, block).transpose(0, 2, 1, 3)
        qtime_blocks = qtime_blocks.reshape(head_count, blocks, tile_rows * block)
        ktime_blocks = split_cols(ktime_tile, group, block, RAD).transpose(0, 2, 1, 3)
        ktime_blocks = ktime_blocks.reshape(head_count, blocks, key_tile_rows * key_tile_cols)
        vtime_blocks = split_cols(vtime_tile, group, block, RAD).transpose(0, 2, 1, 3)
        vtime_blocks = vtime_blocks.reshape(head_count, blocks, key_tile_rows * key_tile_cols)
        cin_blocks = split_cols(cin_tile, group, block, RAD)
        key_valid = rin_tile[:, None, None] & cin_blocks[None]
        key_valid = key_valid.transpose(1, 0, 2).reshape(blocks, key_tile_rows * key_tile_cols)
        inner = jnp.einsum('hbdq,hbdk->hbqk', query_blocks, key_blocks, preferred_element_type=jnp.float32)
        lorentz_dot = inner - qtime_blocks[:, :, :, None] * ktime_blocks[:, :, None, :]
        scores_now = head_scale[:, None, None, None] * (2.0 + 2.0 * lorentz_dot)
        allowed = window_mask[None, None] & key_valid[None, :, None, :]
        scores_now = jnp.where(allowed, scores_now, -jnp.inf)
        peak_score = lax.optimization_barrier(jnp.max(scores_now, axis=-1, keepdims=True))
        weights = jnp.exp(scores_now - peak_score).astype(jnp.bfloat16)
        mean_space = jnp.einsum('hbqk,hbdk->hbdq', weights, value_blocks, preferred_element_type=jnp.float32)
        mean_time = lax.optimization_barrier(jnp.sum(weights.astype(jnp.float32) * vtime_blocks[:, :, None, :], axis=-1))
        spread = jnp.sqrt(mean_time * mean_time - lax.optimization_barrier(jnp.sum(mean_space * mean_space, axis=2)))
        attended = (mean_space / spread[:, :, None, :]).astype(jnp.bfloat16)
        attended = attended.reshape(head_count, blocks, head_width, tile_rows, block).transpose(0, 2, 3, 1, 4)
        return attended.reshape(head_count, head_width, tile_rows, group)
    tiles = lax.map(one_tile, jnp.arange(tile_count, dtype=jnp.int32))
    tiles = tiles.reshape(row_count // tile_rows, col_groups, head_count, head_width, tile_rows, group)
    return tiles.transpose(2, 3, 0, 4, 1, 5).reshape(head_count, head_width, row_count, col_count)

def mix_out(attended, out_weight, token_block):
    head_count, head_width, row_count, col_count = attended.shape
    flattened = attended.reshape(head_count * head_width, row_count * col_count)
    projected = lax.dot_general(flattened, out_weight, (((0,), (0,)), ((), ())), preferred_element_type=jnp.float32)
    projected = projected.reshape(row_count, col_count, head_count * head_width)
    return (token_block.astype(jnp.float32) + projected).astype(jnp.bfloat16)

def pool_scores(pool_queries, key_heads, head_scale):
    head_count, head_width = (key_heads.shape[0], key_heads.shape[1])
    key_flat = key_heads.reshape(head_count, head_width, -1)
    pool_space = pool_queries.astype(jnp.float32).reshape(pool_queries.shape[0], head_count, head_width)
    pool_time = jnp.sqrt(1.0 + lax.optimization_barrier(jnp.sum(pool_space * pool_space, axis=-1)))
    lorentz_dot = jnp.einsum('phd,hdt->pht', pool_space, key_flat.astype(jnp.float32), precision=lax.Precision.HIGHEST)
    lorentz_dot = lorentz_dot - pool_time[:, :, None] * lorentz_time(key_flat)[None]
    return head_scale[None, :, None] * (2.0 + 2.0 * lorentz_dot)

def pool_partial(pool_score, peak_score, value_heads):
    head_count, head_width = (value_heads.shape[0], value_heads.shape[1])
    value_flat = value_heads.reshape(head_count, head_width, -1)
    weights = jnp.exp(pool_score - peak_score[:, :, None])
    mean_space = jnp.einsum('pht,hdt->phd', weights, value_flat.astype(jnp.float32), precision=lax.Precision.HIGHEST)
    mean_time = lax.optimization_barrier(jnp.sum(weights * lorentz_time(value_flat)[None], axis=-1))
    return (mean_space, mean_time)

def finish_pool(mean_space, mean_time):
    spread = jnp.sqrt(mean_time * mean_time - lax.optimization_barrier(jnp.sum(mean_space * mean_space, axis=-1)))
    pooled = mean_space / spread[:, :, None]
    return pooled.reshape(pooled.shape[0], -1)

def reference(tokens, norm_gain, query_weight, key_weight, value_weight, out_weight, head_scale, pool_queries):
    normed = normalize(tokens, norm_gain)
    query_heads = project(query_weight, normed, HEADS)
    key_heads = project(key_weight, normed, HEADS)
    value_heads = project(value_weight, normed, HEADS)
    key_rows = jnp.pad(key_heads, ((0, 0), (0, 0), (RAD, RAD), (0, 0)))
    value_rows = jnp.pad(value_heads, ((0, 0), (0, 0), (RAD, RAD), (0, 0)))

    def one_block(block_index):
        row_start = (block_index * ROWS_DEV).astype(jnp.int32)
        query_block = lax.dynamic_slice_in_dim(query_heads, row_start, ROWS_DEV, 2)
        key_block = lax.dynamic_slice_in_dim(key_rows, row_start, ROWS_DEV + 2 * RAD, 2)
        value_block = lax.dynamic_slice_in_dim(value_rows, row_start, ROWS_DEV + 2 * RAD, 2)
        token_block = lax.dynamic_slice_in_dim(tokens, row_start, ROWS_DEV, 0)
        global_rows = row_start - RAD + jnp.arange(ROWS_DEV + 2 * RAD, dtype=jnp.int32)
        row_inside = (global_rows >= 0) & (global_rows < SLAB_ROWS)
        attended = window_attend(query_block, key_block, value_block, row_inside, head_scale)
        return mix_out(attended, out_weight, token_block)
    block_count = SLAB_ROWS // ROWS_DEV
    mixed = lax.map(one_block, jnp.arange(block_count, dtype=jnp.int32))
    mixed = mixed.reshape(SLAB_ROWS, COLS, D)
    pool_score = pool_scores(pool_queries, key_heads, head_scale)
    peak_score = lax.optimization_barrier(jnp.max(pool_score, axis=-1))
    mean_space, mean_time = pool_partial(pool_score, peak_score, value_heads)
    pooled = finish_pool(mean_space, mean_time)
    return (mixed, pooled)
```

```python
import math

import jax
import jax.numpy as jnp
from jax import lax
from jax.experimental import pallas as pl
from jax.experimental.pallas import tpu as pltpu
from jax.sharding import PartitionSpec as P

RAD = 4
EPS = 1e-06
HEAD = 64
LANES = 128
BLOCK = 32
SPLIT = 6
BIG = 1e30
F32 = jnp.float32
BF16 = jnp.bfloat16
LOG2E = math.log2(math.e)
NT = (((1,), (1,)), ((), ()))


def lane_iota(shape):
    return lax.broadcasted_iota(jnp.int32, shape, len(shape) - 1)


def row_iota(shape):
    return lax.broadcasted_iota(jnp.int32, shape, 0)


def normalize(tokens, gain):
    feats = tokens.astype(F32)
    mean_sq = jnp.mean(feats * feats, axis=-1, keepdims=True)
    return feats * lax.rsqrt(mean_sq + EPS) * gain


def shift_columns(normed, cols):
    rows = normed.shape[0] // cols
    return jnp.concatenate(
        [pltpu.roll(normed[r * cols : (r + 1) * cols], RAD, 0) for r in range(rows)], axis=0
    )


def head_lanes(heads):
    shape = (heads * HEAD, LANES)
    head, lane = row_iota(shape) // HEAD, lane_iota(shape)
    hit = lane == head
    for piece in range(1, SPLIT):
        hit = hit | (lane == head + piece * heads)
    return hit.astype(F32).astype(BF16)


def time_pieces(points, sums):
    f = points.astype(F32)
    sq = f * f
    hi = sq.astype(BF16)
    lo = (sq - hi.astype(F32)).astype(BF16)
    total = jnp.dot(hi, sums, preferred_element_type=F32) + jnp.dot(
        lo, sums, preferred_element_type=F32
    )
    t = jnp.sqrt(1.0 + total)
    first = t.astype(BF16).astype(F32)
    rest = t - first
    second = rest.astype(BF16).astype(F32)
    third = (rest - second).astype(BF16).astype(F32)
    return first, second, third


def query_times(pieces, heads, lane):
    first, second, third = pieces
    mixed = jnp.where((lane >= heads) & (lane < 2 * heads), second, first)
    mixed = jnp.where((lane >= 2 * heads) & (lane < 3 * heads), third, mixed)
    mixed = jnp.where((lane >= 4 * heads) & (lane < 5 * heads), second, mixed)
    return jnp.where(lane < SPLIT * heads, -mixed, 0.0)


def key_times(pieces, heads, lane):
    first, second, third = pieces
    mixed = jnp.where(lane < 3 * heads, first, jnp.where(lane < 5 * heads, second, third))
    return jnp.where(lane < SPLIT * heads, mixed, 0.0)


def value_times(pieces, heads, lane):
    first, second, third = pieces
    mixed = jnp.where(lane < heads, first, jnp.where(lane < 2 * heads, second, third))
    return jnp.where(lane < 3 * heads, mixed, 0.0)


def store_rows(ref, first_row, pitch, cols, value, lanes):
    rows = value.shape[0] // cols
    for r in range(rows):
        base = (first_row + r) * pitch
        row = value[r * cols : (r + 1) * cols]
        ref[base : base + cols, lanes] = row
        ref[base + cols : base + pitch, lanes] = row[: pitch - cols]


def project_strip(normed, k_w, v_w, sums, heads, cols, pitch, first_row, k_ref, v_ref, invalid):
    width = heads * HEAD
    keys = jnp.dot(normed, k_w[...], preferred_element_type=F32).astype(BF16)
    store_rows(k_ref, first_row, pitch, cols, keys, slice(0, width))
    values = jnp.dot(normed, v_w[...], preferred_element_type=F32).astype(BF16)
    store_rows(v_ref, first_row, pitch, cols, values, slice(0, width))
    lane = lane_iota((normed.shape[0], LANES))
    k_time = key_times(time_pieces(keys, sums), heads, lane).astype(BF16)
    v_time = value_times(time_pieces(values, sums), heads, lane).astype(BF16)
    store_rows(v_ref, first_row, pitch, cols, v_time, slice(width, width + LANES))
    flag_lane = SPLIT * heads + BLOCK + RAD
    place = row_iota((pitch, LANES))
    flag = lane_iota((pitch, LANES)) == flag_lane
    outside = (place < RAD) | (place >= cols + RAD)
    if invalid is not None:
        outside = outside | (invalid > 0)
    bias = jnp.where(flag & outside, -BIG, 0.0).astype(BF16)
    for r in range(normed.shape[0] // cols):
        base = (first_row + r) * pitch
        row = k_time[r * cols : (r + 1) * cols]
        row = jnp.concatenate([row, row[: pitch - cols]], axis=0)
        k_ref[base : base + pitch, width : width + LANES] = row + bias


def window_bias(mask_ref, key_rows, wide, first, heads):
    shape = (key_rows * wide, LANES)
    place, lane = row_iota(shape), lane_iota(shape)
    key_row = place // wide
    key_col = place - key_row * wide
    key_row = key_row + first
    col = lane - SPLIT * heads
    row = col - BLOCK
    bad_col = (col >= 0) & (col < BLOCK) & ((key_col < col) | (key_col > col + 2 * RAD))
    bad_row = (row >= 0) & (row < RAD) & ((key_row < row) | (key_row > row + 2 * RAD))
    mask_ref[...] = jnp.where(bad_col | bad_row, -BIG, 0.0).astype(BF16)


def query_features(token_count, cols, heads):
    shape = (token_count, LANES)
    token, lane = row_iota(shape), lane_iota(shape)
    col = lane - SPLIT * heads
    hit = (col == token % BLOCK) & (col < BLOCK)
    hit = hit | (col == BLOCK + token // cols) | (col == BLOCK + RAD)
    return jnp.where(hit & (col >= 0), 1.0, 0.0)


def head_mask(heads, head, lane, pieces):
    hit = lane == head
    for piece in range(1, pieces):
        hit = hit | (lane == piece * heads + head)
    return hit


def window_scores(q_ref, k_ref, mask_ref, block, pair, rows, cols, pitch, wide, key_rows, heads):
    width = heads * HEAD
    lanes = slice(pair * LANES, (pair + 1) * LANES)
    extra = slice(width, width + LANES)
    lane = lane_iota((1, LANES))
    q_start = [pl.multiple_of(r * cols + block * BLOCK, BLOCK) for r in range(rows)]
    q = jnp.concatenate([q_ref[pl.ds(s, BLOCK), lanes] for s in q_start], axis=0)
    qx = jnp.concatenate([q_ref[pl.ds(s, BLOCK), extra] for s in q_start], axis=0)
    stacked = []
    for half in range(2):
        own = (lane < HEAD) if half == 0 else (lane >= HEAD)
        keep = head_mask(heads, 2 * pair + half, lane, SPLIT) | (lane >= SPLIT * heads)
        stacked.append(
            jnp.concatenate(
                [q * own.astype(F32).astype(BF16), qx * keep.astype(F32).astype(BF16)], axis=1
            )
        )
    k_start = [pl.multiple_of(r * pitch + block * BLOCK, 16) for r in range(key_rows)]
    k = jnp.concatenate([k_ref[pl.ds(s, wide), lanes] for s in k_start], axis=0)
    kx = jnp.concatenate([k_ref[pl.ds(s, wide), extra] for s in k_start], axis=0)
    kx = kx + mask_ref[...]
    return lax.dot_general(
        jnp.concatenate(stacked, axis=0),
        jnp.concatenate([k, kx], axis=1),
        NT,
        preferred_element_type=F32,
    )


def weighted_values(weights, v_ref, block, pair, pitch, wide, key_rows, heads):
    width = heads * HEAD
    starts = [pl.multiple_of(r * pitch + block * BLOCK, 16) for r in range(key_rows)]
    v = jnp.concatenate(
        [v_ref[pl.ds(s, wide), pair * LANES : (pair + 1) * LANES] for s in starts], axis=0
    )
    vx = jnp.concatenate([v_ref[pl.ds(s, wide), width : width + LANES] for s in starts], axis=0)
    return jnp.dot(weights, jnp.concatenate([v, vx], axis=1), preferred_element_type=F32)


def window_pass(
    q_ref, k_ref, v_ref, mask_ref, scale_ref, block, pair, rows, cols, pitch, wide, key_rows, heads
):
    scores = window_scores(
        q_ref, k_ref, mask_ref, block, pair, rows, cols, pitch, wide, key_rows, heads
    )
    half = scores.shape[0] // 2
    lane = lane_iota((1, LANES))
    peak = jnp.max(scores, axis=-1, keepdims=True)
    scale = [scale_ref[2 * pair + i] for i in range(2)]
    weights = [
        jnp.exp2((scores[i * half : (i + 1) * half] - peak[i * half : (i + 1) * half]) * scale[i])
        for i in range(2)
    ]
    weights = jnp.concatenate(weights, axis=0).astype(BF16)
    total = weighted_values(weights, v_ref, block, pair, pitch, wide, key_rows, heads)
    space = jnp.where(lane < HEAD, total[:half, :LANES], total[half:, :LANES])
    times = [
        jnp.sum(
            jnp.where(
                head_mask(heads, 2 * pair + i, lane, 3),
                total[i * half : (i + 1) * half, LANES:],
                0.0,
            ),
            axis=-1,
            keepdims=True,
        )
        for i in range(2)
    ]
    return [peak[:half], peak[half:]], space, times


def keys_body(
    parity_ref, scale_ref, own_ref, mate_ref, gain_ref, k_w, v_w, pool_ref, k_ref, v_ref, out_ref
):
    rows_cols, width = own_ref.shape
    heads = width // HEAD
    cols = LANES
    rows = rows_cols // cols
    pitch = k_ref.shape[0] // (2 * rows)
    sums = head_lanes(heads)
    odd = parity_ref[0] > 0
    own, mate = own_ref[...].astype(F32), mate_ref[...].astype(F32)
    for strip in range(2):
        tokens = jnp.where(odd, mate, own) if strip == 0 else jnp.where(odd, own, mate)
        normed = shift_columns(normalize(tokens, gain_ref[...]), cols).astype(BF16)
        project_strip(
            normed, k_w, v_w, sums, heads, cols, pitch, strip * rows, k_ref, v_ref, None
        )
    pq = pool_ref[...]
    count = pq.shape[0]
    lane = lane_iota((count, LANES))
    q_time = query_times(time_pieces(pq, sums), heads, lane)
    zero = jnp.zeros((count, LANES), F32)
    q_rows = []
    for h in range(heads):
        tiles = [zero] * (width // LANES)
        tile = pq[:, h // 2 * LANES : (h // 2 + 1) * LANES].astype(F32)
        tiles[h // 2] = jnp.where((lane < HEAD) if h % 2 == 0 else (lane >= HEAD), tile, 0.0)
        tiles.append(jnp.where(head_mask(heads, h, lane, SPLIT), q_time, 0.0))
        q_rows.append(jnp.concatenate(tiles, axis=1))
    q_all = jnp.concatenate(q_rows, axis=0).astype(BF16)
    keys = jnp.concatenate([k_ref[r * pitch : r * pitch + cols] for r in range(2 * rows)], axis=0)
    scores = lax.dot_general(q_all, keys, NT, preferred_element_type=F32)
    peak = jnp.max(scores, axis=-1, keepdims=True)
    scale = jnp.concatenate(
        [jnp.full((count, 1), scale_ref[h], F32) for h in range(heads)], axis=0
    )
    f = jnp.exp2((scores - peak) * scale)
    hi = f.astype(BF16)
    lo = (f - hi.astype(F32)).astype(BF16)
    values = jnp.concatenate(
        [v_ref[r * pitch : r * pitch + cols] for r in range(2 * rows)], axis=0
    )
    total = jnp.dot(jnp.concatenate([hi, lo], axis=0), values, preferred_element_type=F32)
    total = total[: heads * count] + total[heads * count :]
    stats = zero
    for h in range(heads):
        part = slice(h * count, (h + 1) * count)
        time = jnp.where(head_mask(heads, h, lane, 3), total[part, width:], 0.0)
        stats = jnp.where(lane == h, jnp.sum(time, axis=-1, keepdims=True), stats)
        stats = jnp.where(lane == HEAD + h, peak[part], stats)
    for j in range(width // LANES):
        tile = slice(j * LANES, (j + 1) * LANES)
        first = total[2 * j * count : (2 * j + 1) * count, tile]
        second = total[(2 * j + 1) * count : (2 * j + 2) * count, tile]
        out_ref[j * count : (j + 1) * count, :] = jnp.where(lane < HEAD, first, second)
    out_ref[width // LANES * count :, :] = stats


def near_body(
    parity_ref, scale_ref, own_ref, gain_ref, q_w, k_ref, v_ref, q_ref, space_ref, stat_ref, mask_ref
):
    token_count, width = own_ref.shape
    heads = width // HEAD
    cols = LANES
    rows = token_count // cols
    key_rows = 2 * rows
    pitch = k_ref.shape[0] // key_rows
    wide = mask_ref.shape[0] // key_rows
    normed = normalize(own_ref[...], gain_ref[...]).astype(BF16)
    queries = jnp.dot(normed, q_w[...], preferred_element_type=F32).astype(BF16)
    q_ref[:, :width] = queries
    lane = lane_iota((token_count, LANES))
    extra = query_times(time_pieces(queries, head_lanes(heads)), heads, lane)
    q_ref[:, width:] = (extra + query_features(token_count, cols, heads)).astype(BF16)
    window_bias(mask_ref, key_rows, wide, RAD * (1 - parity_ref[0]), heads)
    stat_lane = lane_iota((1, LANES))

    def one_block(block, carry):
        stats = jnp.zeros((rows * BLOCK, LANES), F32)
        for pair in range(heads // 2):
            peaks, space, times = window_pass(
                q_ref, k_ref, v_ref, mask_ref, scale_ref, block, pair,
                rows, cols, pitch, wide, key_rows, heads,
            )
            space_ref[block, :, pair * LANES : (pair + 1) * LANES] = space
            for i in range(2):
                stats = jnp.where(stat_lane == 2 * pair + i, times[i], stats)
                stats = jnp.where(stat_lane == HEAD + 2 * pair + i, peaks[i], stats)
        stat_ref[block] = stats
        return carry

    lax.fori_loop(0, cols // BLOCK, one_block, 0)


def far_body(
    parity_ref, scale_ref, own_ref, far_ref, gain_ref, k_w, v_w, o_w, q_ref, space_ref, stat_ref,
    out_ref, k_ref, v_ref, mask_ref, mix_ref,
):
    token_count, width = own_ref.shape
    heads = width // HEAD
    cols = LANES
    rows = token_count // cols
    pitch = k_ref.shape[0] // rows
    wide = mask_ref.shape[0] // rows
    normed = shift_columns(normalize(far_ref[...], gain_ref[...]), cols).astype(BF16)
    project_strip(
        normed, k_w, v_w, head_lanes(heads), heads, cols, pitch, 0, k_ref, v_ref, parity_ref[1]
    )
    window_bias(mask_ref, rows, wide, 2 * RAD * parity_ref[0], heads)
    low = lane_iota((1, LANES)) < HEAD

    def one_block(block, carry):
        stats = stat_ref[block]
        for pair in range(heads // 2):
            peaks, space, times = window_pass(
                q_ref, k_ref, v_ref, mask_ref, scale_ref, block, pair,
                rows, cols, pitch, wide, rows, heads,
            )
            h = 2 * pair
            scale = jnp.where(low, scale_ref[h], scale_ref[h + 1])
            near_time = jnp.where(low, stats[:, h : h + 1], stats[:, h + 1 : h + 2])
            near_peak = jnp.where(
                low, stats[:, HEAD + h : HEAD + h + 1], stats[:, HEAD + h + 1 : HEAD + h + 2]
            )
            far_time = jnp.where(low, times[0], times[1])
            far_peak = jnp.where(low, peaks[0], peaks[1])
            peak = jnp.maximum(near_peak, far_peak)
            near = jnp.exp2((near_peak - peak) * scale)
            far = jnp.exp2((far_peak - peak) * scale)
            mean = space_ref[block, :, pair * LANES : (pair + 1) * LANES] * near + space * far
            time = near_time * near + far_time * far
            sq = mean * mean
            norm = jnp.where(
                low,
                jnp.sum(jnp.where(low, sq, 0.0), axis=-1, keepdims=True),
                jnp.sum(jnp.where(low, 0.0, sq), axis=-1, keepdims=True),
            )
            attended = (mean * lax.rsqrt(time * time - norm)).astype(BF16)
            for r in range(rows):
                start = pl.multiple_of(r * cols + block * BLOCK, BLOCK)
                mix_ref[pl.ds(start, BLOCK), pair * LANES : (pair + 1) * LANES] = attended[
                    r * BLOCK : (r + 1) * BLOCK
                ]
        return carry

    lax.fori_loop(0, cols // BLOCK, one_block, 0)
    projected = jnp.dot(mix_ref[...], o_w[...], preferred_element_type=F32)
    out_ref[...] = (own_ref[...].astype(F32) + projected).astype(BF16)


def merge_parts(first, second, scale, count):
    lane = lane_iota((count, LANES))
    tiles = first.shape[0] // count - 1
    s1, s2 = first[tiles * count :], second[tiles * count :]
    peak = jnp.maximum(s1, s2)
    f1 = jnp.exp2(jnp.where(lane >= HEAD, (s1 - peak) * scale, 0.0))
    f2 = jnp.exp2(jnp.where(lane >= HEAD, (s2 - peak) * scale, 0.0))
    time = s1 * pltpu.roll(f1, HEAD, 1) + s2 * pltpu.roll(f2, HEAD, 1)
    stats = jnp.where(lane < HEAD, time, peak)
    spaces = []
    for j in range(tiles):
        part = slice(j * count, (j + 1) * count)
        a, b = HEAD + 2 * j, HEAD + 2 * j + 1
        g1 = jnp.where(lane < HEAD, f1[:, a : a + 1], f1[:, b : b + 1])
        g2 = jnp.where(lane < HEAD, f2[:, a : a + 1], f2[:, b : b + 1])
        spaces.append(first[part] * g1 + second[part] * g2)
    return spaces, stats


def merge_body(upper_ref, scale_ref, mine_ref, other_ref, out_ref, *, count, last):
    upper = upper_ref[0] > 0
    mine, other = mine_ref[...], other_ref[...]
    first, second = jnp.where(upper, other, mine), jnp.where(upper, mine, other)
    spaces, stats = merge_parts(first, second, scale_ref[...], count)
    if not last:
        out_ref[...] = jnp.concatenate(spaces + [stats], axis=0)
        return
    low = lane_iota((count, LANES)) < HEAD
    for j, mean in enumerate(spaces):
        time = jnp.where(low, stats[:, 2 * j : 2 * j + 1], stats[:, 2 * j + 1 : 2 * j + 2])
        sq = mean * mean
        norm = jnp.where(
            low,
            jnp.sum(jnp.where(low, sq, 0.0), axis=-1, keepdims=True),
            jnp.sum(jnp.where(low, 0.0, sq), axis=-1, keepdims=True),
        )
        out_ref[:, j * LANES : (j + 1) * LANES] = mean / jnp.sqrt(time * time - norm)


SMEM = pl.BlockSpec(memory_space=pltpu.SMEM)
VMEM = pl.BlockSpec(memory_space=pltpu.VMEM)


def local_call(body, args, outs, scratch=(), limit=48, name=None):
    specs = [SMEM if a.ndim == 1 else VMEM for a in args]
    out_specs = jax.tree.map(lambda _: VMEM, outs)
    return pl.pallas_call(
        body,
        out_shape=outs,
        in_specs=specs,
        out_specs=out_specs,
        scratch_shapes=list(scratch),
        compiler_params=pltpu.CompilerParams(vmem_limit_bytes=limit << 20),
        name=name,
    )(*args)


def per_device(
    tokens, norm_gain, query_weight, key_weight, value_weight, out_weight, head_scale, pool_queries
):
    rows, cols, width = tokens.shape
    heads = head_scale.shape[0]
    count = pool_queries.shape[0]
    axis = "row"
    ring = lax.axis_size(axis)
    assert rows == RAD and cols == LANES and width == heads * HEAD
    assert ring & (ring - 1) == 0 and ring > 2
    index = lax.axis_index(axis)
    parity = index % 2
    edge = ((index == 0) | (index == ring - 1)).astype(jnp.int32)
    where = jnp.stack([parity, edge]).astype(jnp.int32)
    own = tokens.reshape(rows * cols, width)
    swap = [(i, i ^ 1) for i in range(ring)]
    cross = [(i, i + 1) for i in range(1, ring - 1, 2)] + [
        (i + 1, i) for i in range(1, ring - 1, 2)
    ]
    far = lax.ppermute(own, axis, cross)
    mate = lax.ppermute(own, axis, swap)
    gain = norm_gain.reshape(1, width)
    scale = head_scale * (2.0 * LOG2E)
    near_pitch, near_wide = cols + 16, BLOCK + 16
    far_pitch, far_wide = cols + 32, 2 * BLOCK
    extra = width + LANES
    struct = jax.ShapeDtypeStruct
    keys, values, part = local_call(
        keys_body,
        (where, scale, own, mate, gain, key_weight, value_weight, pool_queries),
        (
            struct((2 * rows * near_pitch, extra), BF16),
            struct((2 * rows * near_pitch, extra), BF16),
            struct(((width // LANES + 1) * count, LANES), F32),
        ),
        name="keys",
    )
    blocks = cols // BLOCK
    queries, space, stat = local_call(
        near_body,
        (where, scale, own, gain, query_weight, keys, values),
        (
            struct((rows * cols, extra), BF16),
            struct((blocks, rows * BLOCK, width), F32),
            struct((blocks, rows * BLOCK, LANES), F32),
        ),
        [pltpu.VMEM((2 * rows * near_wide, LANES), BF16)],
        name="near",
    )
    lane_scale = jnp.zeros((1, LANES), F32).at[0, HEAD : HEAD + heads].set(scale)
    step = 2
    while step < ring:
        other = lax.ppermute(part, axis, [(i, i ^ step) for i in range(ring)])
        upper = ((index // step) % 2).astype(jnp.int32).reshape(1)
        last = 2 * step >= ring
        shape = (count, width) if last else part.shape
        part = local_call(
            lambda *refs, last=last: merge_body(*refs, count=count, last=last),
            (upper, lane_scale, part, other),
            struct(shape, F32),
            limit=8,
            name="merge",
        )
        step *= 2
    mixed = local_call(
        far_body,
        (where, scale, own, far, gain, key_weight, value_weight, out_weight, queries, space, stat),
        struct((rows * cols, width), BF16),
        [
            pltpu.VMEM((rows * far_pitch, extra), BF16),
            pltpu.VMEM((rows * far_pitch, extra), BF16),
            pltpu.VMEM((rows * far_wide, LANES), BF16),
            pltpu.VMEM((rows * cols, width), BF16),
        ],
        name="far",
    )
    return mixed.reshape(rows, cols, width), part


def solution(mesh):
    placed = (P(("slide", "row"), None, None), P(), P(), P(), P(), P(), P(), P())
    return jax.shard_map(
        per_device,
        mesh=mesh,
        in_specs=placed,
        out_specs=(P(("slide", "row"), None, None), P("slide", None)),
        check_vma=False,
    )
```

```python
import math

import jax
import jax.numpy as jnp
from jax import lax
from jax.experimental import pallas as pl
from jax.experimental.pallas import tpu as pltpu
from jax.sharding import PartitionSpec as P


RAD = 4
EPS = 1e-06
HEAD = 64
LANES = 128
BLOCK = 16
WIDE = 2 * BLOCK
SPLIT = 6
BIG = 1e30
F32 = jnp.float32
BF16 = jnp.bfloat16
DOUBLE_LOG2E = 2.0 * math.log2(math.e)
NT = (((1,), (1,)), ((), ()))
AXIS = "row"


def lane_iota(shape):
    return lax.broadcasted_iota(jnp.int32, shape, len(shape) - 1)


def row_iota(shape):
    return lax.broadcasted_iota(jnp.int32, shape, 0)


def normalize(tokens, gain):
    feats = tokens.astype(F32)
    mean_sq = jnp.mean(feats * feats, axis=-1, keepdims=True)
    return feats * lax.rsqrt(mean_sq + EPS) * gain


def shift_columns(normed, cols):
    rows = normed.shape[0] // cols
    return jnp.concatenate(
        [pltpu.roll(normed[r * cols : (r + 1) * cols], RAD, 0) for r in range(rows)], axis=0
    )


def lane_heads(heads):
    lane = lane_iota((1, LANES))
    head = lane
    for piece in range(1, LANES // heads + 1):
        head = jnp.where(lane >= piece * heads, lane - piece * heads, head)
    return head


def value_lane_heads(heads):
    lane = lane_iota((1, LANES))
    high = jnp.where(lane >= HEAD, 1, 0)
    place = lane - HEAD * high
    pairs = heads // 2
    rest = place
    for piece in range(1, 3):
        rest = jnp.where(place >= piece * pairs, place - piece * pairs, rest)
    return jnp.where(place < 3 * pairs, 2 * rest + high, -1)


def value_mask(heads, head):
    lane = lane_iota((1, LANES))
    first = HEAD * (head % 2) + head // 2
    pairs = heads // 2
    return (lane == first) | (lane == first + pairs) | (lane == first + 2 * pairs)


def half_sums(squares):
    low = lane_iota((1, LANES)) < HEAD
    return (
        jnp.sum(jnp.where(low, squares, 0.0), axis=-1, keepdims=True),
        jnp.sum(jnp.where(low, 0.0, squares), axis=-1, keepdims=True),
    )


def time_pieces(points, heads, head):
    total = jnp.zeros((points.shape[0], LANES), F32)
    for j in range(heads // 2):
        f = points[:, j * LANES : (j + 1) * LANES].astype(F32)
        first, second = half_sums(f * f)
        total = jnp.where(head == 2 * j, first, jnp.where(head == 2 * j + 1, second, total))
    t = jnp.sqrt(1.0 + total)
    first = t.astype(BF16).astype(F32)
    rest = t - first
    second = rest.astype(BF16).astype(F32)
    third = (rest - second).astype(BF16).astype(F32)
    return first, second, third


def query_times(pieces, heads):
    first, second, third = pieces
    lane = lane_iota((1, LANES))
    mixed = jnp.where((lane >= heads) & (lane < 2 * heads), second, first)
    mixed = jnp.where((lane >= 2 * heads) & (lane < 3 * heads), third, mixed)
    mixed = jnp.where((lane >= 4 * heads) & (lane < 5 * heads), second, mixed)
    return jnp.where(lane < SPLIT * heads, -mixed, 0.0)


def key_times(pieces, heads):
    first, second, third = pieces
    lane = lane_iota((1, LANES))
    mixed = jnp.where(lane < 3 * heads, first, jnp.where(lane < 5 * heads, second, third))
    return jnp.where(lane < SPLIT * heads, mixed, 0.0)


def value_times(pieces, heads):
    first, second, third = pieces
    lane = lane_iota((1, LANES))
    place = jnp.where(lane >= HEAD, lane - HEAD, lane)
    pairs = heads // 2
    mixed = jnp.where(place < pairs, first, jnp.where(place < 2 * pairs, second, third))
    return jnp.where(place < 3 * pairs, mixed, 0.0)


def store_rows(ref, pitch, cols, value, lane):
    for r in range(value.shape[0] // cols):
        row = value[r * cols : (r + 1) * cols]
        lanes = slice(lane, lane + value.shape[1])
        ref[r * pitch : r * pitch + cols, lanes] = row
        ref[r * pitch + cols : (r + 1) * pitch, lanes] = row[: pitch - cols]


def store_keys(keys, heads, cols, pitch, ref, invalid):
    width = heads * HEAD
    store_rows(ref, pitch, cols, keys, 0)
    times = key_times(time_pieces(keys, heads, lane_heads(heads)), heads)
    place = row_iota((pitch, LANES))
    outside = (place < RAD) | (place >= cols + RAD)
    if invalid is not None:
        outside = outside | invalid
    flag = lane_iota((pitch, LANES)) == SPLIT * heads + BLOCK + RAD
    bias = jnp.where(flag & outside, -BIG, 0.0)
    for r in range(keys.shape[0] // cols):
        row = times[r * cols : (r + 1) * cols]
        row = jnp.concatenate([row, row[: pitch - cols]], axis=0)
        ref[r * pitch : (r + 1) * pitch, width : width + LANES] = (row + bias).astype(BF16)


def store_values(values, heads, cols, pitch, ref):
    width = heads * HEAD
    base = width + LANES
    store_rows(ref, pitch, cols, values, base)
    times = value_times(time_pieces(values, heads, value_lane_heads(heads)), heads).astype(BF16)
    store_rows(ref, pitch, cols, times, base + width)


def window_bias(mask_ref, first, heads):
    shape = mask_ref.shape
    place, lane = row_iota(shape), lane_iota(shape)
    key_row = place // WIDE
    key_col = place - key_row * WIDE
    key_row = key_row + first
    col = lane - SPLIT * heads
    row = col - BLOCK
    bad_col = (col >= 0) & (col < BLOCK) & ((key_col < col) | (key_col > col + 2 * RAD))
    bad_row = (row >= 0) & (row < RAD) & ((key_row < row) | (key_row > row + 2 * RAD))
    mask_ref[...] = jnp.where(bad_col | bad_row, -BIG, 0.0).astype(BF16)


def query_features(cols, heads, row):
    shape = (cols, LANES)
    token, lane = row_iota(shape), lane_iota(shape)
    col = lane - SPLIT * heads
    hit = (col == token % BLOCK) | (col == BLOCK + row) | (col == BLOCK + RAD)
    return jnp.where(hit & (col >= 0), 1.0, 0.0)


def head_mask(heads, head, lane, pieces):
    hit = lane == head
    for piece in range(1, pieces):
        hit = hit | (lane == piece * heads + head)
    return hit


def as_factor(hit):
    return jnp.where(hit, 1.0, 0.0).astype(BF16)


def window_attention(q_ref, kv_refs, mask_ref, scale_ref, heads, finish):
    width = heads * HEAD
    extra = width + LANES
    cols = LANES
    rows = q_ref.shape[0] // cols
    blocks = cols // BLOCK
    pairs = range(heads // 2)
    lane = lane_iota((1, LANES))
    low = lane < HEAD
    sides = [as_factor(low), as_factor(lane >= HEAD)]
    keeps = [
        as_factor(head_mask(heads, h, lane, SPLIT) | (lane >= SPLIT * heads)) for h in range(heads)
    ]
    scale = [scale_ref[h] * DOUBLE_LOG2E for h in range(heads)]
    half = rows * BLOCK
    parts = (slice(0, half), slice(half, 2 * half))

    def queries_of(block, lanes):
        starts = [r * cols + block * BLOCK for r in range(rows)]
        return jnp.concatenate([q_ref[s : s + BLOCK, lanes] for s in starts], axis=0)

    def keys_of(block, lanes):
        tiles = []
        for ref in kv_refs:
            pitch = ref.shape[0] // rows
            starts = [r * pitch + block * BLOCK for r in range(rows)]
            tiles += [ref[s : s + WIDE, lanes] for s in starts]
        return jnp.concatenate(tiles, axis=0)

    def extras(block):
        return (
            queries_of(block, slice(width, extra)),
            keys_of(block, slice(width, extra)) + mask_ref[...],
        )

    def scores_of(block, pair, qx, kx):
        tile = slice(pair * LANES, (pair + 1) * LANES)
        q = queries_of(block, tile)
        stacked = [
            jnp.concatenate([q * sides[i], qx * keeps[2 * pair + i]], axis=1) for i in range(2)
        ]
        return lax.dot_general(
            jnp.concatenate(stacked, axis=0),
            jnp.concatenate([keys_of(block, tile), kx], axis=1),
            NT,
            preferred_element_type=F32,
        )

    extra_now = extras(0)
    scores = [scores_of(0, pair, *extra_now) for pair in pairs]
    behind = None
    for block in range(blocks):
        ahead = extras(block + 1) if block + 1 < blocks else None
        peaks, coming = [], []
        for pair in pairs:
            peaks.append(jnp.max(scores[pair], axis=-1, keepdims=True))
            if ahead is not None:
                coming.append(scores_of(block + 1, pair, *ahead))
        vx = keys_of(block, slice(extra + width, 2 * extra))
        totals = []
        for pair in pairs:
            both = [
                jnp.exp2((scores[pair][part] - peaks[pair][part]) * scale[2 * pair + i])
                for i, part in enumerate(parts)
            ]
            weights = jnp.concatenate(both, axis=0).astype(BF16)
            v = keys_of(block, slice(extra + pair * LANES, extra + (pair + 1) * LANES))
            totals.append(
                jnp.dot(weights, jnp.concatenate([v, vx], axis=1), preferred_element_type=F32)
            )
            if behind is not None:
                finish(block - 1, pair, *behind[pair])
        behind = []
        for pair in pairs:
            total, peak = totals[pair], peaks[pair]
            behind.append(
                (
                    jnp.where(low, peak[parts[0]], peak[parts[1]]),
                    jnp.where(low, total[parts[0], :LANES], total[parts[1], :LANES]),
                    jnp.where(low, total[parts[0], LANES:], total[parts[1], LANES:]),
                    jnp.where(low, scale[2 * pair], scale[2 * pair + 1]),
                )
            )
        scores = coming
    for pair in pairs:
        finish(blocks - 1, pair, *behind[pair])


def project_body(
    gain_ref, own_hbm, q_hbm, k_hbm, v_hbm, kv_ref, q_ref, own_ref, q_w, k_w, v_w, sems
):
    copies = [
        pltpu.make_async_copy(src, dst, sems.at[i])
        for i, (src, dst) in enumerate(
            ((own_hbm, own_ref), (k_hbm, k_w), (v_hbm, v_w), (q_hbm, q_w))
        )
    ]
    for copy in copies:
        copy.start()
    width = own_ref.shape[1]
    heads = width // HEAD
    cols = LANES
    rows = own_ref.shape[0] // cols
    pitch = kv_ref.shape[0] // rows
    copies[0].wait()
    normed = normalize(own_ref[...], gain_ref[...][None, :])
    shifted = shift_columns(normed, cols).astype(BF16)
    normed = normed.astype(BF16)
    copies[1].wait()
    keys = jnp.dot(shifted, k_w[...], preferred_element_type=F32).astype(BF16)
    copies[2].wait()
    values = jnp.dot(shifted, v_w[...], preferred_element_type=F32).astype(BF16)
    store_keys(keys, heads, cols, pitch, kv_ref, None)
    copies[3].wait()
    queries = jnp.dot(normed, q_w[...], preferred_element_type=F32).astype(BF16)
    store_values(values, heads, cols, pitch, kv_ref)
    q_ref[:, :width] = queries
    times = query_times(time_pieces(queries, heads, lane_heads(heads)), heads)
    for r in range(rows):
        part = slice(r * cols, (r + 1) * cols)
        q_ref[part, width:] = (times[part] + query_features(cols, heads, r)).astype(BF16)


def pool_body(scale_ref, pool_ref, kv_ref, out_ref):
    pq = pool_ref[...]
    count, width = pq.shape
    heads = width // HEAD
    cols = LANES
    extra = width + LANES
    pitch = cols + WIDE - BLOCK
    rows = kv_ref.shape[0] // pitch
    lane = lane_iota((count, LANES))
    q_time = query_times(time_pieces(pq, heads, lane_heads(heads)), heads)
    zero = jnp.zeros((count, LANES), F32)
    q_rows = []
    for h in range(heads):
        tiles = [zero] * (width // LANES)
        tile = pq[:, h // 2 * LANES : (h // 2 + 1) * LANES].astype(F32)
        tiles[h // 2] = jnp.where((lane < HEAD) if h % 2 == 0 else (lane >= HEAD), tile, 0.0)
        tiles.append(jnp.where(head_mask(heads, h, lane, SPLIT), q_time, 0.0))
        q_rows.append(jnp.concatenate(tiles, axis=1))
    q_all = jnp.concatenate(q_rows, axis=0).astype(BF16)
    keys = jnp.concatenate(
        [kv_ref[r * pitch : r * pitch + cols, :extra] for r in range(rows)], axis=0
    )
    scores = lax.dot_general(q_all, keys, NT, preferred_element_type=F32)
    peak = jnp.max(scores, axis=-1, keepdims=True)
    scale = jnp.concatenate(
        [jnp.full((count, 1), scale_ref[h] * DOUBLE_LOG2E, F32) for h in range(heads)], axis=0
    )
    f = jnp.exp2((scores - peak) * scale)
    hi = f.astype(BF16)
    lo = (f - hi.astype(F32)).astype(BF16)
    values = jnp.concatenate(
        [kv_ref[r * pitch : r * pitch + cols, extra:] for r in range(rows)], axis=0
    )
    total = jnp.dot(jnp.concatenate([hi, lo], axis=0), values, preferred_element_type=F32)
    total = total[: heads * count] + total[heads * count :]
    stats = zero
    for h in range(heads):
        part = slice(h * count, (h + 1) * count)
        time = jnp.where(value_mask(heads, h), total[part, width:], 0.0)
        stats = jnp.where(lane == h, jnp.sum(time, axis=-1, keepdims=True), stats)
        stats = jnp.where(lane == HEAD + h, peak[part], stats)
    for j in range(width // LANES):
        tile = slice(j * LANES, (j + 1) * LANES)
        first = total[2 * j * count : (2 * j + 1) * count, tile]
        second = total[(2 * j + 1) * count : (2 * j + 2) * count, tile]
        out_ref[j * count : (j + 1) * count, :] = jnp.where(lane < HEAD, first, second)
    out_ref[width // LANES * count :, :] = stats


def near_body(scale_ref, q_ref, own_ref, mate_ref, peak_ref, space_ref, time_ref, mask_ref):
    width = q_ref.shape[1] - LANES
    heads = width // HEAD
    size = q_ref.shape[0] // LANES * BLOCK
    half = mask_ref.shape[0] // 2
    odd = lax.axis_index(AXIS) % 2
    window_bias(mask_ref.at[:half], RAD, heads)
    window_bias(mask_ref.at[half:], 2 * RAD * (1 - odd), heads)
    mine = [value_mask(heads, 2 * j) | value_mask(heads, 2 * j + 1) for j in range(heads // 2)]
    block_times = {}

    def finish(block, pair, peak, space, times, scale):
        part = slice(block * size, (block + 1) * size)
        tile = slice(pair * LANES, (pair + 1) * LANES)
        peak_ref[part, tile] = peak
        space_ref[part, tile] = space
        so_far = block_times.get(block)
        times = times if so_far is None else jnp.where(mine[pair], times, so_far)
        block_times[block] = times
        if pair == heads // 2 - 1:
            time_ref[part, :] = times

    window_attention(q_ref, (own_ref, mate_ref), mask_ref, scale_ref, heads, finish)


def far_body(
    scale_ref, gain_ref, far_ref, k_w, v_w, o_w, own_ref, q_ref, peak_ref, space_ref, time_ref,
    out_ref, kv_ref, mask_ref, mix_ref,
):
    width = own_ref.shape[1]
    heads = width // HEAD
    cols = LANES
    rows = own_ref.shape[0] // cols
    size = rows * BLOCK
    pitch = kv_ref.shape[0] // rows
    index = lax.axis_index(AXIS)
    odd = index % 2
    invalid = (index == 0) | (index == lax.axis_size(AXIS) - 1)
    window_bias(mask_ref, 2 * RAD * odd, heads)
    shifted = normalize(far_ref[...], gain_ref[...][None, :])
    shifted = shift_columns(shifted, cols).astype(BF16)
    keys = jnp.dot(shifted, k_w[...], preferred_element_type=F32).astype(BF16)
    values = jnp.dot(shifted, v_w[...], preferred_element_type=F32).astype(BF16)
    store_keys(keys, heads, cols, pitch, kv_ref, invalid)
    store_values(values, heads, cols, pitch, kv_ref)
    low = lane_iota((1, LANES)) < HEAD
    mine = [value_mask(heads, 2 * j) | value_mask(heads, 2 * j + 1) for j in range(heads // 2)]

    def finish(block, pair, far_peak, far_space, far_times, scale):
        part = slice(block * size, (block + 1) * size)
        tile = slice(pair * LANES, (pair + 1) * LANES)
        near_peak = peak_ref[part, tile]
        peak = jnp.maximum(near_peak, far_peak)
        near = jnp.exp2((near_peak - peak) * scale)
        far = jnp.exp2((far_peak - peak) * scale)
        mean = space_ref[part, tile] * near + far_space * far
        times = jnp.where(mine[pair], time_ref[part, :] * near + far_times * far, 0.0)
        time = jnp.where(low, *half_sums(times))
        spread = time * time - jnp.where(low, *half_sums(mean * mean))
        attended = (mean * lax.rsqrt(spread)).astype(BF16)
        for r in range(rows):
            start = r * cols + block * BLOCK
            mix_ref[start : start + BLOCK, tile] = attended[r * BLOCK : (r + 1) * BLOCK]

    window_attention(q_ref, (kv_ref,), mask_ref, scale_ref, heads, finish)
    projected = jnp.dot(mix_ref[...], o_w[...], preferred_element_type=F32)
    out_ref[...] = (own_ref[...].astype(F32) + projected).astype(BF16)


def merge_body(scale_ref, mine_ref, other_ref, out_ref, *, count, step, last):
    upper = (lax.axis_index(AXIS) // step) % 2 > 0
    mine, other = mine_ref[...], other_ref[...]
    first, second = jnp.where(upper, other, mine), jnp.where(upper, mine, other)
    lane = lane_iota((count, LANES))
    low = lane < HEAD
    tiles = first.shape[0] // count - 1
    scale = jnp.zeros((count, LANES), F32)
    for h in range(2 * tiles):
        scale = jnp.where(lane == HEAD + h, scale_ref[h] * DOUBLE_LOG2E, scale)
    s1, s2 = first[tiles * count :], second[tiles * count :]
    peak = jnp.maximum(s1, s2)
    f1 = jnp.exp2((s1 - peak) * scale)
    f2 = jnp.exp2((s2 - peak) * scale)
    time = s1 * pltpu.roll(f1, HEAD, 1) + s2 * pltpu.roll(f2, HEAD, 1)
    stats = jnp.where(low, time, peak)
    for j in range(tiles):
        part = slice(j * count, (j + 1) * count)
        a, b = HEAD + 2 * j, HEAD + 2 * j + 1
        g1 = jnp.where(low, f1[:, a : a + 1], f1[:, b : b + 1])
        g2 = jnp.where(low, f2[:, a : a + 1], f2[:, b : b + 1])
        mean = first[part] * g1 + second[part] * g2
        if not last:
            out_ref[part, :] = mean
            continue
        time = jnp.where(low, stats[:, 2 * j : 2 * j + 1], stats[:, 2 * j + 1 : 2 * j + 2])
        one, two = half_sums(mean * mean)
        out_ref[:, j * LANES : (j + 1) * LANES] = mean / jnp.sqrt(
            time * time - jnp.where(low, one, two)
        )
    if not last:
        out_ref[tiles * count :, :] = stats


SMEM = pl.BlockSpec(memory_space=pltpu.SMEM)
VMEM = pl.BlockSpec(memory_space=pltpu.VMEM)
HBM = pl.BlockSpec(memory_space=pltpu.HBM)


def local_call(body, specs, args, outs, scratch=(), limit=24):
    return pl.pallas_call(
        body,
        out_shape=outs,
        in_specs=list(specs),
        out_specs=jax.tree.map(lambda _: VMEM, outs),
        scratch_shapes=list(scratch),
        compiler_params=pltpu.CompilerParams(vmem_limit_bytes=limit << 20),
    )(*args)


def exchange(value, pairs):
    return lax.ppermute(value, AXIS, pairs)


def per_device(
    tokens, norm_gain, query_weight, key_weight, value_weight, out_weight, head_scale, pool_queries
):
    rows, cols, width = tokens.shape
    heads = head_scale.shape[0]
    count = pool_queries.shape[0]
    ring = lax.axis_size(AXIS)
    assert rows == RAD and cols == LANES and width == heads * HEAD
    assert ring & (ring - 1) == 0 and ring > 1
    struct = jax.ShapeDtypeStruct
    cells = rows * cols
    own = tokens.reshape(cells, width)
    swap = [(i, i ^ 1) for i in range(ring)]
    cross = [(i, i + 1) for i in range(1, ring - 1, 2)]
    cross = cross + [(b, a) for a, b in cross]
    far = exchange(own, cross)
    extra = width + LANES
    pitch = cols + WIDE - BLOCK
    keys_values, queries = local_call(
        project_body,
        (VMEM, HBM, HBM, HBM, HBM),
        (norm_gain, own, query_weight, key_weight, value_weight),
        (struct((rows * pitch, 2 * extra), BF16), struct((cells, extra), BF16)),
        [pltpu.VMEM((cells, width), BF16)]
        + [pltpu.VMEM((width, width), BF16)] * 3
        + [pltpu.SemaphoreType.DMA((4,))],
        limit=60,
    )
    mate = exchange(keys_values, swap)
    part = local_call(
        pool_body,
        (SMEM, VMEM, VMEM),
        (head_scale, pool_queries, keys_values),
        struct(((width // LANES + 1) * count, LANES), F32),
    )
    near = local_call(
        near_body,
        (SMEM, VMEM, VMEM, VMEM),
        (head_scale, queries, keys_values, mate),
        (
            struct((cells, width), F32),
            struct((cells, width), F32),
            struct((cells, LANES), F32),
        ),
        [pltpu.VMEM((2 * rows * WIDE, LANES), BF16)],
    )
    for hop in range(ring.bit_length() - 1):
        step = 1 << hop
        other = exchange(part, [(i, i ^ step) for i in range(ring)])
        last = 2 * step >= ring
        part = local_call(
            lambda *refs, step=step, last=last: merge_body(
                *refs, count=count, step=step, last=last
            ),
            (SMEM, VMEM, VMEM),
            (head_scale, part, other),
            struct((count, width) if last else part.shape, F32),
            limit=4,
        )
    mixed = local_call(
        far_body,
        (SMEM,) + (VMEM,) * 10,
        (head_scale, norm_gain, far, key_weight, value_weight, out_weight, own, queries, *near),
        struct((cells, width), BF16),
        [
            pltpu.VMEM((rows * pitch, 2 * extra), BF16),
            pltpu.VMEM((rows * WIDE, LANES), BF16),
            pltpu.VMEM((cells, width), BF16),
        ],
    )
    return mixed.reshape(rows, cols, width), part


def solution(mesh):
    placed = (P(("slide", "row"), None, None), P(), P(), P(), P(), P(), P(), P())
    return jax.shard_map(
        per_device,
        mesh=mesh,
        in_specs=placed,
        out_specs=(P(("slide", "row"), None, None), P("slide", None)),
        check_vma=False,
    )
```

```python
import math

import jax
import jax.numpy as jnp
from jax import lax
from jax.experimental import pallas as pl
from jax.experimental.pallas import tpu as pltpu
from jax.sharding import PartitionSpec as P


RAD = 4
EPS = 1e-06
HEAD = 64
LANES = 128
BLOCK = 16
WIDE = 2 * BLOCK
SPLIT = 6
BIG = 1e30
F32 = jnp.float32
BF16 = jnp.bfloat16
DOUBLE_LOG2E = 2.0 * math.log2(math.e)
NT = (((1,), (1,)), ((), ()))
AXIS = "row"


def lane_iota(shape):
    return lax.broadcasted_iota(jnp.int32, shape, len(shape) - 1)


def row_iota(shape):
    return lax.broadcasted_iota(jnp.int32, shape, 0)


def normalize(tokens, gain):
    feats = tokens.astype(F32)
    mean_sq = jnp.mean(feats * feats, axis=-1, keepdims=True)
    return feats * lax.rsqrt(mean_sq + EPS) * gain


def shift_columns(normed, cols):
    rows = normed.shape[0] // cols
    return jnp.concatenate(
        [pltpu.roll(normed[r * cols : (r + 1) * cols], RAD, 0) for r in range(rows)], axis=0
    )


def lane_heads(heads):
    lane = lane_iota((1, LANES))
    head = lane
    for piece in range(1, LANES // heads + 1):
        head = jnp.where(lane >= piece * heads, lane - piece * heads, head)
    return head


def value_lane_heads(heads):
    lane = lane_iota((1, LANES))
    high = jnp.where(lane >= HEAD, 1, 0)
    place = lane - HEAD * high
    pairs = heads // 2
    rest = place
    for piece in range(1, 3):
        rest = jnp.where(place >= piece * pairs, place - piece * pairs, rest)
    return jnp.where(place < 3 * pairs, 2 * rest + high, -1)


def value_mask(heads, head):
    lane = lane_iota((1, LANES))
    first = HEAD * (head % 2) + head // 2
    pairs = heads // 2
    return (lane == first) | (lane == first + pairs) | (lane == first + 2 * pairs)


def half_sums(squares):
    low = lane_iota((1, LANES)) < HEAD
    return (
        jnp.sum(jnp.where(low, squares, 0.0), axis=-1, keepdims=True),
        jnp.sum(jnp.where(low, 0.0, squares), axis=-1, keepdims=True),
    )


def time_pieces(points, heads, head, matmul_tiles=0):
    tiles = heads // 2
    split = (tiles - matmul_tiles) * LANES
    total = jnp.zeros((points.shape[0], LANES), F32)
    if matmul_tiles:
        f = points[:, split:].astype(F32)
        sq = f * f
        hi = sq.astype(BF16)
        lo = (sq - hi.astype(F32)).astype(BF16)
        hit = row_iota((sq.shape[1], LANES)) // HEAD + split // HEAD == head
        sums = as_factor(hit)
        total = jnp.dot(hi, sums, preferred_element_type=F32)
        total = total + jnp.dot(lo, sums, preferred_element_type=F32)
    for j in range(tiles - matmul_tiles):
        f = points[:, j * LANES : (j + 1) * LANES].astype(F32)
        first, second = half_sums(f * f)
        total = jnp.where(head == 2 * j, first, jnp.where(head == 2 * j + 1, second, total))
    t = jnp.sqrt(1.0 + total)
    first = t.astype(BF16).astype(F32)
    rest = t - first
    second = rest.astype(BF16).astype(F32)
    third = (rest - second).astype(BF16).astype(F32)
    return first, second, third


def query_times(pieces, heads):
    first, second, third = pieces
    lane = lane_iota((1, LANES))
    mixed = jnp.where((lane >= heads) & (lane < 2 * heads), second, first)
    mixed = jnp.where((lane >= 2 * heads) & (lane < 3 * heads), third, mixed)
    mixed = jnp.where((lane >= 4 * heads) & (lane < 5 * heads), second, mixed)
    return jnp.where(lane < SPLIT * heads, -mixed, 0.0)


def key_times(pieces, heads):
    first, second, third = pieces
    lane = lane_iota((1, LANES))
    mixed = jnp.where(lane < 3 * heads, first, jnp.where(lane < 5 * heads, second, third))
    return jnp.where(lane < SPLIT * heads, mixed, 0.0)


def value_times(pieces, heads):
    first, second, third = pieces
    lane = lane_iota((1, LANES))
    place = jnp.where(lane >= HEAD, lane - HEAD, lane)
    pairs = heads // 2
    mixed = jnp.where(place < pairs, first, jnp.where(place < 2 * pairs, second, third))
    return jnp.where(place < 3 * pairs, mixed, 0.0)


def store_rows(ref, pitch, cols, value, lane):
    for r in range(value.shape[0] // cols):
        row = value[r * cols : (r + 1) * cols]
        lanes = slice(lane, lane + value.shape[1])
        ref[r * pitch : r * pitch + cols, lanes] = row
        ref[r * pitch + cols : (r + 1) * pitch, lanes] = row[: pitch - cols]


def store_keys(keys, heads, cols, pitch, ref, invalid):
    width = heads * HEAD
    store_rows(ref, pitch, cols, keys, 0)
    times = key_times(time_pieces(keys, heads, lane_heads(heads)), heads)
    place = row_iota((pitch, LANES))
    outside = (place < RAD) | (place >= cols + RAD)
    if invalid is not None:
        outside = outside | invalid
    flag = lane_iota((pitch, LANES)) == SPLIT * heads + BLOCK + RAD
    bias = jnp.where(flag & outside, -BIG, 0.0)
    for r in range(keys.shape[0] // cols):
        row = times[r * cols : (r + 1) * cols]
        row = jnp.concatenate([row, row[: pitch - cols]], axis=0)
        ref[r * pitch : (r + 1) * pitch, width : width + LANES] = (row + bias).astype(BF16)


def store_values(values, heads, cols, pitch, ref):
    width = heads * HEAD
    base = width + LANES
    store_rows(ref, pitch, cols, values, base)
    times = value_times(time_pieces(values, heads, value_lane_heads(heads), heads // 4), heads).astype(BF16)
    store_rows(ref, pitch, cols, times, base + width)


def window_bias(mask_ref, first, heads):
    shape = mask_ref.shape
    place, lane = row_iota(shape), lane_iota(shape)
    key_row = place // WIDE
    key_col = place - key_row * WIDE
    key_row = key_row + first
    col = lane - SPLIT * heads
    row = col - BLOCK
    bad_col = (col >= 0) & (col < BLOCK) & ((key_col < col) | (key_col > col + 2 * RAD))
    bad_row = (row >= 0) & (row < RAD) & ((key_row < row) | (key_row > row + 2 * RAD))
    mask_ref[...] = jnp.where(bad_col | bad_row, -BIG, 0.0).astype(BF16)


def query_features(cols, heads, row):
    shape = (cols, LANES)
    token, lane = row_iota(shape), lane_iota(shape)
    col = lane - SPLIT * heads
    hit = (col == token % BLOCK) | (col == BLOCK + row) | (col == BLOCK + RAD)
    return jnp.where(hit & (col >= 0), 1.0, 0.0)


def head_mask(heads, head, lane, pieces):
    hit = lane == head
    for piece in range(1, pieces):
        hit = hit | (lane == piece * heads + head)
    return hit


def as_factor(hit):
    return jnp.where(hit, 1.0, 0.0).astype(BF16)


def window_attention(q_ref, kv_refs, mask_ref, scale_ref, heads, blocks, finish):
    width = heads * HEAD
    extra = width + LANES
    cols = LANES
    rows = q_ref.shape[0] // cols
    pairs = range(heads // 2)
    lane = lane_iota((1, LANES))
    low = lane < HEAD
    sides = [as_factor(low), as_factor(lane >= HEAD)]
    keeps = [
        as_factor(head_mask(heads, h, lane, SPLIT) | (lane >= SPLIT * heads)) for h in range(heads)
    ]
    scale = [scale_ref[h] * DOUBLE_LOG2E for h in range(heads)]
    half = rows * BLOCK
    parts = (slice(0, half), slice(half, 2 * half))

    def queries_of(block, lanes):
        starts = [r * cols + block * BLOCK for r in range(rows)]
        return jnp.concatenate([q_ref[s : s + BLOCK, lanes] for s in starts], axis=0)

    def keys_of(block, lanes):
        tiles = []
        for ref in kv_refs:
            pitch = ref.shape[0] // rows
            starts = [r * pitch + block * BLOCK for r in range(rows)]
            tiles += [ref[s : s + WIDE, lanes] for s in starts]
        return jnp.concatenate(tiles, axis=0)

    def extras(block):
        return (
            queries_of(block, slice(width, extra)),
            keys_of(block, slice(width, extra)) + mask_ref[...],
        )

    def scores_of(block, pair, qx, kx):
        tile = slice(pair * LANES, (pair + 1) * LANES)
        q = queries_of(block, tile)
        stacked = [
            jnp.concatenate([q * sides[i], qx * keeps[2 * pair + i]], axis=1) for i in range(2)
        ]
        return lax.dot_general(
            jnp.concatenate(stacked, axis=0),
            jnp.concatenate([keys_of(block, tile), kx], axis=1),
            NT,
            preferred_element_type=F32,
        )

    first, last = blocks[0], blocks[-1]
    extra_now = extras(first)
    scores = [scores_of(first, pair, *extra_now) for pair in pairs]
    behind = None
    for block in blocks:
        ahead = extras(block + 1) if block < last else None
        peaks, coming = [], []
        for pair in pairs:
            peaks.append(jnp.max(scores[pair], axis=-1, keepdims=True))
            if ahead is not None:
                coming.append(scores_of(block + 1, pair, *ahead))
        vx = keys_of(block, slice(extra + width, 2 * extra))
        totals = []
        for pair in pairs:
            both = [
                jnp.exp2((scores[pair][part] - peaks[pair][part]) * scale[2 * pair + i])
                for i, part in enumerate(parts)
            ]
            weights = jnp.concatenate(both, axis=0).astype(BF16)
            v = keys_of(block, slice(extra + pair * LANES, extra + (pair + 1) * LANES))
            totals.append(
                jnp.dot(weights, jnp.concatenate([v, vx], axis=1), preferred_element_type=F32)
            )
            if behind is not None:
                finish(block - 1, pair, *behind[pair])
        behind = []
        for pair in pairs:
            total, peak = totals[pair], peaks[pair]
            behind.append(
                (
                    jnp.where(low, peak[parts[0]], peak[parts[1]]),
                    jnp.where(low, total[parts[0], :LANES], total[parts[1], :LANES]),
                    jnp.where(low, total[parts[0], LANES:], total[parts[1], LANES:]),
                    jnp.where(low, scale[2 * pair], scale[2 * pair + 1]),
                )
            )
        scores = coming
    for pair in pairs:
        finish(last, pair, *behind[pair])


def project_body(gain_hbm, own_hbm, k_hbm, v_hbm, kv_ref, normed_ref, gain_ref, own_ref, k_w, v_w, sems):
    cells, width = own_ref.shape
    heads = width // HEAD
    cols = LANES
    rows = cells // cols
    pitch = kv_ref.shape[0] // rows
    strips = [slice(r * cols, (r + 1) * cols) for r in range(rows)]
    moves = [(gain_hbm, gain_ref)] + [(own_hbm.at[part], own_ref.at[part]) for part in strips]
    moves += [(k_hbm, k_w), (v_hbm, v_w)]
    copies = [pltpu.make_async_copy(src, dst, sems.at[i]) for i, (src, dst) in enumerate(moves)]
    for copy in copies:
        copy.start()
    copies[0].wait()
    gain = gain_ref[...][None, :]
    shifted = []
    for r, part in enumerate(strips):
        copies[1 + r].wait()
        normed = normalize(own_ref[part], gain)
        normed_ref[part] = normed.astype(BF16)
        shifted.append(pltpu.roll(normed, RAD, 0).astype(BF16))
    shifted = jnp.concatenate(shifted, axis=0)
    copies[-2].wait()
    keys = jnp.dot(shifted, k_w[...], preferred_element_type=F32).astype(BF16)
    copies[-1].wait()
    values = jnp.dot(shifted, v_w[...], preferred_element_type=F32).astype(BF16)
    store_keys(keys, heads, cols, pitch, kv_ref, None)
    store_values(values, heads, cols, pitch, kv_ref)


def query_body(scale_ref, pool_ref, normed_ref, q_hbm, kv_ref, q_ref, out_ref, q_w, sem):
    copy = pltpu.make_async_copy(q_hbm, q_w, sem)
    copy.start()
    pq = pool_ref[...]
    count, width = pq.shape
    heads = width // HEAD
    cols = LANES
    extra = width + LANES
    rows = q_ref.shape[0] // cols
    pitch = kv_ref.shape[0] // rows
    lane = lane_iota((count, LANES))
    q_time = query_times(time_pieces(pq, heads, lane_heads(heads)), heads)
    zero = jnp.zeros((count, LANES), F32)
    q_rows = []
    for h in range(heads):
        tiles = [zero] * (width // LANES)
        tile = pq[:, h // 2 * LANES : (h // 2 + 1) * LANES].astype(F32)
        tiles[h // 2] = jnp.where((lane < HEAD) if h % 2 == 0 else (lane >= HEAD), tile, 0.0)
        tiles.append(jnp.where(head_mask(heads, h, lane, SPLIT), q_time, 0.0))
        q_rows.append(jnp.concatenate(tiles, axis=1))
    q_all = jnp.concatenate(q_rows, axis=0).astype(BF16)
    keys = jnp.concatenate(
        [kv_ref[r * pitch : r * pitch + cols, :extra] for r in range(rows)], axis=0
    )
    copy.wait()
    queries = jnp.dot(normed_ref[...], q_w[...], preferred_element_type=F32).astype(BF16)
    q_ref[:, :width] = queries
    scores = lax.dot_general(q_all, keys, NT, preferred_element_type=F32)
    times = query_times(time_pieces(queries, heads, lane_heads(heads)), heads)
    for r in range(rows):
        part = slice(r * cols, (r + 1) * cols)
        q_ref[part, width:] = (times[part] + query_features(cols, heads, r)).astype(BF16)
    scale = jnp.concatenate(
        [jnp.full((count, 1), scale_ref[h] * DOUBLE_LOG2E, F32) for h in range(heads)], axis=0
    )
    scores = scores * scale
    peak = jnp.max(scores, axis=-1, keepdims=True)
    f = jnp.exp2(scores - peak)
    hi = f.astype(BF16)
    lo = (f - hi.astype(F32)).astype(BF16)
    values = jnp.concatenate(
        [kv_ref[r * pitch : r * pitch + cols, extra:] for r in range(rows)], axis=0
    )
    total = jnp.dot(jnp.concatenate([hi, lo], axis=0), values, preferred_element_type=F32)
    total = total[: heads * count] + total[heads * count :]
    stats = zero
    for h in range(heads):
        part = slice(h * count, (h + 1) * count)
        time = jnp.where(value_mask(heads, h), total[part, width:], 0.0)
        stats = jnp.where(lane == h, jnp.sum(time, axis=-1, keepdims=True), stats)
        stats = jnp.where(lane == HEAD + h, peak[part], stats)
    for j in range(width // LANES):
        tile = slice(j * LANES, (j + 1) * LANES)
        first = total[2 * j * count : (2 * j + 1) * count, tile]
        second = total[(2 * j + 1) * count : (2 * j + 2) * count, tile]
        out_ref[j * count : (j + 1) * count, :] = jnp.where(lane < HEAD, first, second)
    out_ref[width // LANES * count :, :] = stats


def near_body(scale_ref, q_ref, own_ref, mate_ref, peak_ref, space_ref, time_ref, mask_ref, *, blocks):
    width = q_ref.shape[1] - LANES
    heads = width // HEAD
    size = q_ref.shape[0] // LANES * BLOCK
    half = mask_ref.shape[0] // 2
    odd = lax.axis_index(AXIS) % 2
    window_bias(mask_ref.at[:half], RAD, heads)
    window_bias(mask_ref.at[half:], 2 * RAD * (1 - odd), heads)
    mine = [value_mask(heads, 2 * j) | value_mask(heads, 2 * j + 1) for j in range(heads // 2)]
    block_times = {}

    def finish(block, pair, peak, space, times, scale):
        place = block - blocks[0]
        part = slice(place * size, (place + 1) * size)
        tile = slice(pair * LANES, (pair + 1) * LANES)
        peak_ref[part, tile] = peak
        space_ref[part, tile] = space
        so_far = block_times.get(block)
        times = times if so_far is None else jnp.where(mine[pair], times, so_far)
        block_times[block] = times
        if pair == heads // 2 - 1:
            time_ref[part, :] = times

    window_attention(q_ref, (own_ref, mate_ref), mask_ref, scale_ref, heads, blocks, finish)


def far_body(
    scale_ref, gain_ref, far_ref, k_w, v_w, o_w, own_ref, q_ref,
    peak_a, space_a, time_a, peak_b, space_b, time_b, out_ref, kv_ref, mask_ref, mix_ref,
):
    width = own_ref.shape[1]
    heads = width // HEAD
    cols = LANES
    rows = own_ref.shape[0] // cols
    size = rows * BLOCK
    pitch = kv_ref.shape[0] // rows
    index = lax.axis_index(AXIS)
    odd = index % 2
    invalid = (index == 0) | (index == lax.axis_size(AXIS) - 1)
    window_bias(mask_ref, 2 * RAD * odd, heads)
    shifted = normalize(far_ref[...], gain_ref[...][None, :])
    shifted = shift_columns(shifted, cols).astype(BF16)
    keys = jnp.dot(shifted, k_w[...], preferred_element_type=F32).astype(BF16)
    values = jnp.dot(shifted, v_w[...], preferred_element_type=F32).astype(BF16)
    store_keys(keys, heads, cols, pitch, kv_ref, invalid)
    store_values(values, heads, cols, pitch, kv_ref)
    low = lane_iota((1, LANES)) < HEAD
    mine = [value_mask(heads, 2 * j) | value_mask(heads, 2 * j + 1) for j in range(heads // 2)]

    def finish(block, pair, far_peak, far_space, far_times, scale):
        second = block * size >= peak_a.shape[0]
        peak_ref, space_ref, time_ref = (
            (peak_b, space_b, time_b) if second else (peak_a, space_a, time_a)
        )
        place = block * size - (peak_a.shape[0] if second else 0)
        part = slice(place, place + size)
        tile = slice(pair * LANES, (pair + 1) * LANES)
        near_peak = peak_ref[part, tile]
        peak = jnp.maximum(near_peak, far_peak)
        near = jnp.exp2((near_peak - peak) * scale)
        far = jnp.exp2((far_peak - peak) * scale)
        mean = space_ref[part, tile] * near + far_space * far
        times = jnp.where(mine[pair], time_ref[part, :] * near + far_times * far, 0.0)
        time = jnp.where(low, *half_sums(times))
        spread = time * time - jnp.where(low, *half_sums(mean * mean))
        attended = (mean * lax.rsqrt(spread)).astype(BF16)
        for r in range(rows):
            start = r * cols + block * BLOCK
            mix_ref[start : start + BLOCK, tile] = attended[r * BLOCK : (r + 1) * BLOCK]

    window_attention(q_ref, (kv_ref,), mask_ref, scale_ref, heads, range(cols // BLOCK), finish)
    projected = jnp.dot(mix_ref[...], o_w[...], preferred_element_type=F32)
    out_ref[...] = (own_ref[...].astype(F32) + projected).astype(BF16)


def merge_body(mine_ref, other_ref, out_ref, *, count, step, last):
    upper = (lax.axis_index(AXIS) // step) % 2 > 0
    mine, other = mine_ref[...], other_ref[...]
    first, second = jnp.where(upper, other, mine), jnp.where(upper, mine, other)
    lane = lane_iota((count, LANES))
    low = lane < HEAD
    tiles = first.shape[0] // count - 1
    s1, s2 = first[tiles * count :], second[tiles * count :]
    peak = jnp.maximum(s1, s2)
    f1 = jnp.exp2(jnp.where(low, 0.0, s1 - peak))
    f2 = jnp.exp2(jnp.where(low, 0.0, s2 - peak))
    time = s1 * pltpu.roll(f1, HEAD, 1) + s2 * pltpu.roll(f2, HEAD, 1)
    stats = jnp.where(low, time, peak)
    for j in range(tiles):
        part = slice(j * count, (j + 1) * count)
        a, b = HEAD + 2 * j, HEAD + 2 * j + 1
        g1 = jnp.where(low, f1[:, a : a + 1], f1[:, b : b + 1])
        g2 = jnp.where(low, f2[:, a : a + 1], f2[:, b : b + 1])
        mean = first[part] * g1 + second[part] * g2
        if not last:
            out_ref[part, :] = mean
            continue
        time = jnp.where(low, stats[:, 2 * j : 2 * j + 1], stats[:, 2 * j + 1 : 2 * j + 2])
        one, two = half_sums(mean * mean)
        out_ref[:, j * LANES : (j + 1) * LANES] = mean / jnp.sqrt(
            time * time - jnp.where(low, one, two)
        )
    if not last:
        out_ref[tiles * count :, :] = stats


SMEM = pl.BlockSpec(memory_space=pltpu.SMEM)
VMEM = pl.BlockSpec(memory_space=pltpu.VMEM)
HBM = pl.BlockSpec(memory_space=pltpu.HBM)


def local_call(body, specs, args, outs, scratch=(), limit=24):
    return pl.pallas_call(
        body,
        out_shape=outs,
        in_specs=list(specs),
        out_specs=jax.tree.map(lambda _: VMEM, outs),
        scratch_shapes=list(scratch),
        compiler_params=pltpu.CompilerParams(vmem_limit_bytes=limit << 20),
    )(*args)


def exchange(value, pairs):
    return lax.ppermute(value, AXIS, pairs)


def per_device(
    tokens, norm_gain, query_weight, key_weight, value_weight, out_weight, head_scale, pool_queries
):
    rows, cols, width = tokens.shape
    heads = head_scale.shape[0]
    count = pool_queries.shape[0]
    ring = lax.axis_size(AXIS)
    assert rows == RAD and cols == LANES and width == heads * HEAD
    assert ring & (ring - 1) == 0 and ring > 8
    struct = jax.ShapeDtypeStruct
    cells = rows * cols
    own = tokens.reshape(cells, width)
    swap = [(i, i ^ 1) for i in range(ring)]
    cross = [(i, i + 1) for i in range(1, ring - 1, 2)]
    cross = cross + [(b, a) for a, b in cross]
    far = exchange(own, cross)
    extra = width + LANES
    pitch = cols + WIDE - BLOCK
    in_hbm = [
        pltpu.with_memory_space_constraint(a, pltpu.HBM)
        for a in (norm_gain, own, key_weight, value_weight, query_weight)
    ]
    keys_values, normed = local_call(
        project_body,
        (HBM,) * 4,
        in_hbm[:4],
        (struct((rows * pitch, 2 * extra), BF16), struct((cells, width), BF16)),
        [pltpu.VMEM((width,), F32), pltpu.VMEM((cells, width), BF16)]
        + [pltpu.VMEM((width, width), BF16)] * 2
        + [pltpu.SemaphoreType.DMA((3 + rows,))],
    )
    mate = exchange(keys_values, swap)
    queries, part = local_call(
        query_body,
        (SMEM, VMEM, VMEM, HBM, VMEM),
        (head_scale, pool_queries, normed, in_hbm[4], keys_values),
        (
            struct((cells, extra), BF16),
            struct(((width // LANES + 1) * count, LANES), F32),
        ),
        [pltpu.VMEM((width, width), BF16), pltpu.SemaphoreType.DMA(())],
    )
    near = []
    split = cols // BLOCK // 2
    for blocks in (range(split), range(split, 2 * split)):
        size = split * rows * BLOCK
        near += local_call(
            lambda *refs, blocks=blocks: near_body(*refs, blocks=blocks),
            (SMEM, VMEM, VMEM, VMEM),
            (head_scale, queries, keys_values, mate),
            (
                struct((size, width), F32),
                struct((size, width), F32),
                struct((size, LANES), F32),
            ),
            [pltpu.VMEM((2 * rows * WIDE, LANES), BF16)],
        )
    for hop in range(ring.bit_length() - 1):
        step = 1 << hop
        other = exchange(part, [(i, i ^ step) for i in range(ring)])
        last = 2 * step >= ring
        part = local_call(
            lambda *refs, step=step, last=last: merge_body(
                *refs, count=count, step=step, last=last
            ),
            (VMEM, VMEM),
            (part, other),
            struct((count, width) if last else part.shape, F32),
            limit=4,
        )
    mixed = local_call(
        far_body,
        (SMEM,) + (VMEM,) * 13,
        (head_scale, norm_gain, far, key_weight, value_weight, out_weight, own, queries, *near),
        struct((cells, width), BF16),
        [
            pltpu.VMEM((rows * pitch, 2 * extra), BF16),
            pltpu.VMEM((rows * WIDE, LANES), BF16),
            pltpu.VMEM((cells, width), BF16),
        ],
    )
    return mixed.reshape(rows, cols, width), part


def solution(mesh):
    placed = (P(("slide", "row"), None, None), P(), P(), P(), P(), P(), P(), P())
    return jax.shard_map(
        per_device,
        mesh=mesh,
        in_specs=placed,
        out_specs=(P(("slide", "row"), None, None), P("slide", None)),
        check_vma=False,
    )
```

```python
import math

import jax
import jax.numpy as jnp
from jax import lax
from jax.experimental import pallas as pl
from jax.experimental.pallas import tpu as pltpu
from jax.sharding import PartitionSpec as P


RAD = 4
EPS = 1e-06
HEAD = 64
LANES = 128
BLOCK = 16
WIDE = 2 * BLOCK
SPLIT = 6
BIG = 1e30
F32 = jnp.float32
BF16 = jnp.bfloat16
DOUBLE_LOG2E = 2.0 * math.log2(math.e)
NT = (((1,), (1,)), ((), ()))
AXIS = "row"


def lane_iota(shape):
    return lax.broadcasted_iota(jnp.int32, shape, len(shape) - 1)


def row_iota(shape):
    return lax.broadcasted_iota(jnp.int32, shape, 0)


def normalize(tokens, gain):
    feats = tokens.astype(F32)
    mean_sq = jnp.mean(feats * feats, axis=-1, keepdims=True)
    return feats * lax.rsqrt(mean_sq + EPS) * gain


def shift_columns(normed, cols):
    rows = normed.shape[0] // cols
    return jnp.concatenate(
        [pltpu.roll(normed[r * cols : (r + 1) * cols], RAD, 0) for r in range(rows)], axis=0
    )


def lane_heads(heads):
    lane = lane_iota((1, LANES))
    head = lane
    for piece in range(1, LANES // heads + 1):
        head = jnp.where(lane >= piece * heads, lane - piece * heads, head)
    return head


def value_lane_heads(heads):
    lane = lane_iota((1, LANES))
    high = jnp.where(lane >= HEAD, 1, 0)
    place = lane - HEAD * high
    pairs = heads // 2
    rest = place
    for piece in range(1, 3):
        rest = jnp.where(place >= piece * pairs, place - piece * pairs, rest)
    return jnp.where(place < 3 * pairs, 2 * rest + high, -1)


def value_mask(heads, head):
    lane = lane_iota((1, LANES))
    first = HEAD * (head % 2) + head // 2
    pairs = heads // 2
    return (lane == first) | (lane == first + pairs) | (lane == first + 2 * pairs)


def half_sums(squares):
    low = lane_iota((1, LANES)) < HEAD
    return (
        jnp.sum(jnp.where(low, squares, 0.0), axis=-1, keepdims=True),
        jnp.sum(jnp.where(low, 0.0, squares), axis=-1, keepdims=True),
    )


def time_pieces(points, heads, head, matmul_tiles=0):
    tiles = heads // 2
    split = (tiles - matmul_tiles) * LANES
    total = jnp.zeros((points.shape[0], LANES), F32)
    if matmul_tiles:
        f = points[:, split:].astype(F32)
        sq = f * f
        hi = sq.astype(BF16)
        lo = (sq - hi.astype(F32)).astype(BF16)
        hit = row_iota((sq.shape[1], LANES)) // HEAD + split // HEAD == head
        sums = as_factor(hit)
        total = jnp.dot(hi, sums, preferred_element_type=F32)
        total = total + jnp.dot(lo, sums, preferred_element_type=F32)
    for j in range(tiles - matmul_tiles):
        f = points[:, j * LANES : (j + 1) * LANES].astype(F32)
        first, second = half_sums(f * f)
        total = jnp.where(head == 2 * j, first, jnp.where(head == 2 * j + 1, second, total))
    total = 1.0 + total
    t = total * lax.rsqrt(total)
    first = t.astype(BF16).astype(F32)
    rest = t - first
    second = rest.astype(BF16).astype(F32)
    third = (rest - second).astype(BF16).astype(F32)
    return first, second, third


def query_times(pieces, heads):
    first, second, third = pieces
    lane = lane_iota((1, LANES))
    mixed = jnp.where((lane >= heads) & (lane < 2 * heads), second, first)
    mixed = jnp.where((lane >= 2 * heads) & (lane < 3 * heads), third, mixed)
    mixed = jnp.where((lane >= 4 * heads) & (lane < 5 * heads), second, mixed)
    return jnp.where(lane < SPLIT * heads, -mixed, 0.0)


def key_times(pieces, heads):
    first, second, third = pieces
    lane = lane_iota((1, LANES))
    mixed = jnp.where(lane < 3 * heads, first, jnp.where(lane < 5 * heads, second, third))
    return jnp.where(lane < SPLIT * heads, mixed, 0.0)


def value_times(pieces, heads):
    first, second, third = pieces
    lane = lane_iota((1, LANES))
    place = jnp.where(lane >= HEAD, lane - HEAD, lane)
    pairs = heads // 2
    mixed = jnp.where(place < pairs, first, jnp.where(place < 2 * pairs, second, third))
    return jnp.where(place < 3 * pairs, mixed, 0.0)


def store_rows(ref, pitch, cols, value, lane):
    for r in range(value.shape[0] // cols):
        row = value[r * cols : (r + 1) * cols]
        lanes = slice(lane, lane + value.shape[1])
        ref[r * pitch : r * pitch + cols, lanes] = row
        ref[r * pitch + cols : (r + 1) * pitch, lanes] = row[: pitch - cols]


def store_keys(keys, heads, cols, pitch, ref, invalid):
    width = heads * HEAD
    store_rows(ref, pitch, cols, keys, 0)
    times = key_times(time_pieces(keys, heads, lane_heads(heads)), heads)
    place = row_iota((pitch, LANES))
    outside = (place < RAD) | (place >= cols + RAD)
    if invalid is not None:
        outside = outside | invalid
    flag = lane_iota((pitch, LANES)) == SPLIT * heads + BLOCK + RAD
    bias = jnp.where(flag & outside, -BIG, 0.0)
    for r in range(keys.shape[0] // cols):
        row = times[r * cols : (r + 1) * cols]
        row = jnp.concatenate([row, row[: pitch - cols]], axis=0)
        ref[r * pitch : (r + 1) * pitch, width : width + LANES] = (row + bias).astype(BF16)


def store_values(values, heads, cols, pitch, ref):
    width = heads * HEAD
    base = width + LANES
    store_rows(ref, pitch, cols, values, base)
    times = value_times(time_pieces(values, heads, value_lane_heads(heads), heads // 4), heads).astype(BF16)
    store_rows(ref, pitch, cols, times, base + width)


def window_bias(mask_ref, first, heads):
    shape = mask_ref.shape
    place, lane = row_iota(shape), lane_iota(shape)
    key_row = place // WIDE
    key_col = place - key_row * WIDE
    key_row = key_row + first
    col = lane - SPLIT * heads
    row = col - BLOCK
    bad_col = (col >= 0) & (col < BLOCK) & ((key_col < col) | (key_col > col + 2 * RAD))
    bad_row = (row >= 0) & (row < RAD) & ((key_row < row) | (key_row > row + 2 * RAD))
    mask_ref[...] = jnp.where(bad_col | bad_row, -BIG, 0.0).astype(BF16)


def query_features(cols, heads, row):
    shape = (cols, LANES)
    token, lane = row_iota(shape), lane_iota(shape)
    col = lane - SPLIT * heads
    hit = (col == token % BLOCK) | (col == BLOCK + row) | (col == BLOCK + RAD)
    return jnp.where(hit & (col >= 0), 1.0, 0.0)


def head_mask(heads, head, lane, pieces):
    hit = lane == head
    for piece in range(1, pieces):
        hit = hit | (lane == piece * heads + head)
    return hit


def as_factor(hit):
    return jnp.where(hit, 1.0, 0.0).astype(BF16)


def window_attention(q_ref, kv_refs, mask_ref, scale_ref, heads, blocks, finish):
    width = heads * HEAD
    extra = width + LANES
    cols = LANES
    rows = q_ref.shape[0] // cols
    pairs = range(heads // 2)
    lane = lane_iota((1, LANES))
    low = lane < HEAD
    sides = [as_factor(low), as_factor(lane >= HEAD)]
    keeps = [
        as_factor(head_mask(heads, h, lane, SPLIT) | (lane >= SPLIT * heads)) for h in range(heads)
    ]
    scale = [scale_ref[h] * DOUBLE_LOG2E for h in range(heads)]
    half = rows * BLOCK
    parts = (slice(0, half), slice(half, 2 * half))

    def queries_of(block, lanes):
        starts = [r * cols + block * BLOCK for r in range(rows)]
        return jnp.concatenate([q_ref[s : s + BLOCK, lanes] for s in starts], axis=0)

    def keys_of(block, lanes):
        tiles = []
        for ref in kv_refs:
            pitch = ref.shape[0] // rows
            starts = [r * pitch + block * BLOCK for r in range(rows)]
            tiles += [ref[s : s + WIDE, lanes] for s in starts]
        return jnp.concatenate(tiles, axis=0)

    def extras(block):
        return (
            queries_of(block, slice(width, extra)),
            keys_of(block, slice(width, extra)) + mask_ref[...],
        )

    def scores_of(block, pair, qx, kx):
        tile = slice(pair * LANES, (pair + 1) * LANES)
        q = queries_of(block, tile)
        stacked = [
            jnp.concatenate([q * sides[i], qx * keeps[2 * pair + i]], axis=1) for i in range(2)
        ]
        return lax.dot_general(
            jnp.concatenate(stacked, axis=0),
            jnp.concatenate([keys_of(block, tile), kx], axis=1),
            NT,
            preferred_element_type=F32,
        )

    first, last = blocks[0], blocks[-1]
    extra_now = extras(first)
    scores = [scores_of(first, pair, *extra_now) for pair in pairs]
    behind = None
    for block in blocks:
        ahead = extras(block + 1) if block < last else None
        peaks, coming = [], []
        for pair in pairs:
            peaks.append(jnp.max(scores[pair], axis=-1, keepdims=True))
            if ahead is not None:
                coming.append(scores_of(block + 1, pair, *ahead))
        vx = keys_of(block, slice(extra + width, 2 * extra))
        totals = []
        for pair in pairs:
            both = [
                jnp.exp2((scores[pair][part] - peaks[pair][part]) * scale[2 * pair + i])
                for i, part in enumerate(parts)
            ]
            weights = jnp.concatenate(both, axis=0).astype(BF16)
            v = keys_of(block, slice(extra + pair * LANES, extra + (pair + 1) * LANES))
            totals.append(
                jnp.dot(weights, jnp.concatenate([v, vx], axis=1), preferred_element_type=F32)
            )
            if behind is not None:
                finish(block - 1, pair, *behind[pair])
        behind = []
        for pair in pairs:
            total, peak = totals[pair], peaks[pair]
            behind.append(
                (
                    jnp.where(low, peak[parts[0]], peak[parts[1]]),
                    jnp.where(low, total[parts[0], :LANES], total[parts[1], :LANES]),
                    jnp.where(low, total[parts[0], LANES:], total[parts[1], LANES:]),
                    jnp.where(low, scale[2 * pair], scale[2 * pair + 1]),
                )
            )
        scores = coming
    for pair in pairs:
        finish(last, pair, *behind[pair])


def project_body(gain_hbm, own_hbm, k_hbm, v_hbm, kv_ref, normed_ref, gain_ref, own_ref, k_w, v_w, sems):
    cells, width = own_ref.shape
    heads = width // HEAD
    cols = LANES
    rows = cells // cols
    pitch = kv_ref.shape[0] // rows
    strips = [slice(r * cols, (r + 1) * cols) for r in range(rows)]
    moves = [(gain_hbm, gain_ref)] + [(own_hbm.at[part], own_ref.at[part]) for part in strips]
    moves += [(k_hbm, k_w), (v_hbm, v_w)]
    copies = [pltpu.make_async_copy(src, dst, sems.at[i]) for i, (src, dst) in enumerate(moves)]
    for copy in copies:
        copy.start()
    copies[0].wait()
    gain = gain_ref[...][None, :]
    shifted = []
    for r, part in enumerate(strips):
        copies[1 + r].wait()
        normed = normalize(own_ref[part], gain)
        normed_ref[part] = normed.astype(BF16)
        shifted.append(pltpu.roll(normed, RAD, 0).astype(BF16))
    shifted = jnp.concatenate(shifted, axis=0)
    copies[-2].wait()
    keys = jnp.dot(shifted, k_w[...], preferred_element_type=F32).astype(BF16)
    copies[-1].wait()
    values = jnp.dot(shifted, v_w[...], preferred_element_type=F32).astype(BF16)
    store_keys(keys, heads, cols, pitch, kv_ref, None)
    store_values(values, heads, cols, pitch, kv_ref)


def query_body(scale_ref, pool_ref, normed_ref, q_w, kv_ref, q_ref, out_ref):
    pq = pool_ref[...]
    count, width = pq.shape
    heads = width // HEAD
    cols = LANES
    extra = width + LANES
    rows = q_ref.shape[0] // cols
    pitch = kv_ref.shape[0] // rows
    lane = lane_iota((count, LANES))
    q_time = query_times(time_pieces(pq, heads, lane_heads(heads)), heads)
    zero = jnp.zeros((count, LANES), F32)
    q_rows = []
    for h in range(heads):
        tiles = [zero] * (width // LANES)
        tile = pq[:, h // 2 * LANES : (h // 2 + 1) * LANES].astype(F32)
        tiles[h // 2] = jnp.where((lane < HEAD) if h % 2 == 0 else (lane >= HEAD), tile, 0.0)
        tiles.append(jnp.where(head_mask(heads, h, lane, SPLIT), q_time, 0.0))
        q_rows.append(jnp.concatenate(tiles, axis=1))
    q_all = jnp.concatenate(q_rows, axis=0).astype(BF16)
    keys = jnp.concatenate(
        [kv_ref[r * pitch : r * pitch + cols, :extra] for r in range(rows)], axis=0
    )
    queries = jnp.dot(normed_ref[...], q_w[...], preferred_element_type=F32).astype(BF16)
    q_ref[:, :width] = queries
    scores = lax.dot_general(q_all, keys, NT, preferred_element_type=F32)
    times = query_times(time_pieces(queries, heads, lane_heads(heads)), heads)
    for r in range(rows):
        part = slice(r * cols, (r + 1) * cols)
        q_ref[part, width:] = (times[part] + query_features(cols, heads, r)).astype(BF16)
    scale = jnp.concatenate(
        [jnp.full((count, 1), scale_ref[h] * DOUBLE_LOG2E, F32) for h in range(heads)], axis=0
    )
    scores = scores * scale
    peak = jnp.max(scores, axis=-1, keepdims=True)
    f = jnp.exp2(scores - peak)
    hi = f.astype(BF16)
    lo = (f - hi.astype(F32)).astype(BF16)
    values = jnp.concatenate(
        [kv_ref[r * pitch : r * pitch + cols, extra:] for r in range(rows)], axis=0
    )
    total = jnp.dot(jnp.concatenate([hi, lo], axis=0), values, preferred_element_type=F32)
    total = total[: heads * count] + total[heads * count :]
    stats = zero
    for h in range(heads):
        part = slice(h * count, (h + 1) * count)
        time = jnp.where(value_mask(heads, h), total[part, width:], 0.0)
        stats = jnp.where(lane == h, jnp.sum(time, axis=-1, keepdims=True), stats)
        stats = jnp.where(lane == HEAD + h, peak[part], stats)
    for j in range(width // LANES):
        tile = slice(j * LANES, (j + 1) * LANES)
        first = total[2 * j * count : (2 * j + 1) * count, tile]
        second = total[(2 * j + 1) * count : (2 * j + 2) * count, tile]
        out_ref[j * count : (j + 1) * count, :] = jnp.where(lane < HEAD, first, second)
    out_ref[width // LANES * count :, :] = stats


def near_body(scale_ref, q_ref, own_ref, mate_ref, peak_ref, space_ref, time_ref, mask_ref, *, blocks):
    width = q_ref.shape[1] - LANES
    heads = width // HEAD
    size = q_ref.shape[0] // LANES * BLOCK
    half = mask_ref.shape[0] // 2
    odd = lax.axis_index(AXIS) % 2
    window_bias(mask_ref.at[:half], RAD, heads)
    window_bias(mask_ref.at[half:], 2 * RAD * (1 - odd), heads)
    mine = [value_mask(heads, 2 * j) | value_mask(heads, 2 * j + 1) for j in range(heads // 2)]
    block_times = {}

    def finish(block, pair, peak, space, times, scale):
        place = block - blocks[0]
        part = slice(place * size, (place + 1) * size)
        tile = slice(pair * LANES, (pair + 1) * LANES)
        peak_ref[part, tile] = peak
        space_ref[part, tile] = space
        so_far = block_times.get(block)
        times = times if so_far is None else jnp.where(mine[pair], times, so_far)
        block_times[block] = times
        if pair == heads // 2 - 1:
            time_ref[part, :] = times

    window_attention(q_ref, (own_ref, mate_ref), mask_ref, scale_ref, heads, blocks, finish)


def far_body(
    scale_ref, gain_ref, far_ref, k_w, v_w, o_w, own_ref, q_ref,
    peak_a, space_a, time_a, peak_b, space_b, time_b, out_ref, kv_ref, mask_ref, mix_ref,
):
    width = own_ref.shape[1]
    heads = width // HEAD
    cols = LANES
    rows = own_ref.shape[0] // cols
    size = rows * BLOCK
    pitch = kv_ref.shape[0] // rows
    index = lax.axis_index(AXIS)
    odd = index % 2
    invalid = (index == 0) | (index == lax.axis_size(AXIS) - 1)
    window_bias(mask_ref, 2 * RAD * odd, heads)
    shifted = normalize(far_ref[...], gain_ref[...][None, :])
    shifted = shift_columns(shifted, cols).astype(BF16)
    keys = jnp.dot(shifted, k_w[...], preferred_element_type=F32).astype(BF16)
    values = jnp.dot(shifted, v_w[...], preferred_element_type=F32).astype(BF16)
    store_keys(keys, heads, cols, pitch, kv_ref, invalid)
    store_values(values, heads, cols, pitch, kv_ref)
    low = lane_iota((1, LANES)) < HEAD
    mine = [value_mask(heads, 2 * j) | value_mask(heads, 2 * j + 1) for j in range(heads // 2)]

    def finish(block, pair, far_peak, far_space, far_times, scale):
        second = block * size >= peak_a.shape[0]
        peak_ref, space_ref, time_ref = (
            (peak_b, space_b, time_b) if second else (peak_a, space_a, time_a)
        )
        place = block * size - (peak_a.shape[0] if second else 0)
        part = slice(place, place + size)
        tile = slice(pair * LANES, (pair + 1) * LANES)
        near_peak = peak_ref[part, tile]
        peak = jnp.maximum(near_peak, far_peak)
        near = jnp.exp2((near_peak - peak) * scale)
        far = jnp.exp2((far_peak - peak) * scale)
        mean = space_ref[part, tile] * near + far_space * far
        times = jnp.where(mine[pair], time_ref[part, :] * near + far_times * far, 0.0)
        time = jnp.where(low, *half_sums(times))
        spread = time * time - jnp.where(low, *half_sums(mean * mean))
        attended = (mean * lax.rsqrt(spread)).astype(BF16)
        for r in range(rows):
            start = r * cols + block * BLOCK
            mix_ref[start : start + BLOCK, tile] = attended[r * BLOCK : (r + 1) * BLOCK]

    window_attention(q_ref, (kv_ref,), mask_ref, scale_ref, heads, range(cols // BLOCK), finish)
    projected = jnp.dot(mix_ref[...], o_w[...], preferred_element_type=F32)
    out_ref[...] = (own_ref[...].astype(F32) + projected).astype(BF16)


def merge_body(mine_ref, other_ref, out_ref, *, count, step, last):
    upper = (lax.axis_index(AXIS) // step) % 2 > 0
    mine, other = mine_ref[...], other_ref[...]
    first, second = jnp.where(upper, other, mine), jnp.where(upper, mine, other)
    lane = lane_iota((count, LANES))
    low = lane < HEAD
    tiles = first.shape[0] // count - 1
    s1, s2 = first[tiles * count :], second[tiles * count :]
    peak = jnp.maximum(s1, s2)
    f1 = jnp.exp2(jnp.where(low, 0.0, s1 - peak))
    f2 = jnp.exp2(jnp.where(low, 0.0, s2 - peak))
    time = s1 * pltpu.roll(f1, HEAD, 1) + s2 * pltpu.roll(f2, HEAD, 1)
    stats = jnp.where(low, time, peak)
    for j in range(tiles):
        part = slice(j * count, (j + 1) * count)
        a, b = HEAD + 2 * j, HEAD + 2 * j + 1
        g1 = jnp.where(low, f1[:, a : a + 1], f1[:, b : b + 1])
        g2 = jnp.where(low, f2[:, a : a + 1], f2[:, b : b + 1])
        mean = first[part] * g1 + second[part] * g2
        if not last:
            out_ref[part, :] = mean
            continue
        time = jnp.where(low, stats[:, 2 * j : 2 * j + 1], stats[:, 2 * j + 1 : 2 * j + 2])
        one, two = half_sums(mean * mean)
        out_ref[:, j * LANES : (j + 1) * LANES] = mean / jnp.sqrt(
            time * time - jnp.where(low, one, two)
        )
    if not last:
        out_ref[tiles * count :, :] = stats


SMEM = pl.BlockSpec(memory_space=pltpu.SMEM)
VMEM = pl.BlockSpec(memory_space=pltpu.VMEM)
HBM = pl.BlockSpec(memory_space=pltpu.HBM)


def local_call(body, specs, args, outs, scratch=(), limit=24):
    return pl.pallas_call(
        body,
        out_shape=outs,
        in_specs=list(specs),
        out_specs=jax.tree.map(lambda _: VMEM, outs),
        scratch_shapes=list(scratch),
        compiler_params=pltpu.CompilerParams(vmem_limit_bytes=limit << 20),
    )(*args)


def hop_steps(ring):
    return [1] + [1 << bit for bit in range(2, ring.bit_length() - 1)] + [2]


def exchange(value, pairs):
    return lax.ppermute(value, AXIS, pairs)


def per_device(
    tokens, norm_gain, query_weight, key_weight, value_weight, out_weight, head_scale, pool_queries
):
    rows, cols, width = tokens.shape
    heads = head_scale.shape[0]
    count = pool_queries.shape[0]
    ring = lax.axis_size(AXIS)
    assert rows == RAD and cols == LANES and width == heads * HEAD
    assert ring & (ring - 1) == 0 and ring > 8
    struct = jax.ShapeDtypeStruct
    cells = rows * cols
    own = tokens.reshape(cells, width)
    swap = [(i, i ^ 1) for i in range(ring)]
    cross = [(i, i + 1) for i in range(1, ring - 1, 2)]
    cross = cross + [(b, a) for a, b in cross]
    far = exchange(own, cross)
    extra = width + LANES
    pitch = cols + WIDE - BLOCK
    in_hbm = [
        pltpu.with_memory_space_constraint(a, pltpu.HBM)
        for a in (norm_gain, own, key_weight, value_weight)
    ]
    keys_values, normed = local_call(
        project_body,
        (HBM,) * 4,
        in_hbm,
        (struct((rows * pitch, 2 * extra), BF16), struct((cells, width), BF16)),
        [pltpu.VMEM((width,), F32), pltpu.VMEM((cells, width), BF16)]
        + [pltpu.VMEM((width, width), BF16)] * 2
        + [pltpu.SemaphoreType.DMA((3 + rows,))],
    )
    mate = exchange(keys_values, swap)
    queries, part = local_call(
        query_body,
        (SMEM,) + (VMEM,) * 4,
        (head_scale, pool_queries, normed, query_weight, keys_values),
        (
            struct((cells, extra), BF16),
            struct(((width // LANES + 1) * count, LANES), F32),
        ),
    )
    near = []
    split = cols // BLOCK // 2
    for blocks in (range(split), range(split, 2 * split)):
        size = split * rows * BLOCK
        near += local_call(
            lambda *refs, blocks=blocks: near_body(*refs, blocks=blocks),
            (SMEM, VMEM, VMEM, VMEM),
            (head_scale, queries, keys_values, mate),
            (
                struct((size, width), F32),
                struct((size, width), F32),
                struct((size, LANES), F32),
            ),
            [pltpu.VMEM((2 * rows * WIDE, LANES), BF16)],
        )
    steps = hop_steps(ring)
    for hop, step in enumerate(steps):
        other = exchange(part, [(i, i ^ step) for i in range(ring)])
        last = hop == len(steps) - 1
        part = local_call(
            lambda *refs, step=step, last=last: merge_body(
                *refs, count=count, step=step, last=last
            ),
            (VMEM, VMEM),
            (part, other),
            struct((count, width) if last else part.shape, F32),
            limit=4,
        )
    mixed = local_call(
        far_body,
        (SMEM,) + (VMEM,) * 13,
        (head_scale, norm_gain, far, key_weight, value_weight, out_weight, own, queries, *near),
        struct((cells, width), BF16),
        [
            pltpu.VMEM((rows * pitch, 2 * extra), BF16),
            pltpu.VMEM((rows * WIDE, LANES), BF16),
            pltpu.VMEM((cells, width), BF16),
        ],
    )
    return mixed.reshape(rows, cols, width), part


def solution(mesh):
    placed = (P(("slide", "row"), None, None), P(), P(), P(), P(), P(), P(), P())
    return jax.shard_map(
        per_device,
        mesh=mesh,
        in_specs=placed,
        out_specs=(P(("slide", "row"), None, None), P("slide", None)),
        check_vma=False,
    )
```

```python
import functools
import math

import jax
import jax.numpy as jnp
from jax import lax
from jax.experimental import pallas as pl
from jax.experimental.pallas import tpu as pltpu
from jax.sharding import PartitionSpec as P


RAD = 4
EPS = 1e-06
HEAD = 64
LANES = 128
BLOCK = 16
WIDE = 2 * BLOCK
SPLIT = 6
BIG = 1e30
F32 = jnp.float32
BF16 = jnp.bfloat16
DOUBLE_LOG2E = 2.0 * math.log2(math.e)
NT = (((1,), (1,)), ((), ()))
AXIS = "row"


def lane_iota(shape):
    return lax.broadcasted_iota(jnp.int32, shape, len(shape) - 1)


def row_iota(shape):
    return lax.broadcasted_iota(jnp.int32, shape, 0)


def normalize(tokens, gain):
    feats = tokens.astype(F32)
    mean_sq = jnp.mean(feats * feats, axis=-1, keepdims=True)
    return feats * lax.rsqrt(mean_sq + EPS) * gain


def lane_heads(heads):
    lane = lane_iota((1, LANES))
    head = lane
    for piece in range(1, LANES // heads + 1):
        head = jnp.where(lane >= piece * heads, lane - piece * heads, head)
    return head


def value_lane_heads(heads):
    lane = lane_iota((1, LANES))
    high = jnp.where(lane >= HEAD, 1, 0)
    place = lane - HEAD * high
    pairs = heads // 2
    rest = place
    for piece in range(1, 3):
        rest = jnp.where(place >= piece * pairs, place - piece * pairs, rest)
    return jnp.where(place < 3 * pairs, 2 * rest + high, -1)


def value_mask(heads, head):
    lane = lane_iota((1, LANES))
    first = HEAD * (head % 2) + head // 2
    pairs = heads // 2
    return (lane == first) | (lane == first + pairs) | (lane == first + 2 * pairs)


def half_sums(squares):
    low = lane_iota((1, LANES)) < HEAD
    return (
        jnp.sum(jnp.where(low, squares, 0.0), axis=-1, keepdims=True),
        jnp.sum(jnp.where(low, 0.0, squares), axis=-1, keepdims=True),
    )


def time_pieces(points, heads, head, matmul_tiles=0):
    tiles = heads // 2
    split = (tiles - matmul_tiles) * LANES
    total = jnp.zeros((points.shape[0], LANES), F32)
    if matmul_tiles:
        f = points[:, split:].astype(F32)
        sq = f * f
        hi = sq.astype(BF16)
        lo = (sq - hi.astype(F32)).astype(BF16)
        hit = row_iota((sq.shape[1], LANES)) // HEAD + split // HEAD == head
        sums = as_factor(hit)
        total = jnp.dot(hi, sums, preferred_element_type=F32)
        total = total + jnp.dot(lo, sums, preferred_element_type=F32)
    for j in range(tiles - matmul_tiles):
        f = points[:, j * LANES : (j + 1) * LANES].astype(F32)
        first, second = half_sums(f * f)
        total = jnp.where(head == 2 * j, first, jnp.where(head == 2 * j + 1, second, total))
    total = 1.0 + total
    t = total * lax.rsqrt(total)
    first = t.astype(BF16).astype(F32)
    rest = t - first
    second = rest.astype(BF16).astype(F32)
    third = (rest - second).astype(BF16).astype(F32)
    return first, second, third


def query_times(pieces, heads):
    first, second, third = pieces
    lane = lane_iota((1, LANES))
    mixed = jnp.where((lane >= heads) & (lane < 2 * heads), second, first)
    mixed = jnp.where((lane >= 2 * heads) & (lane < 3 * heads), third, mixed)
    mixed = jnp.where((lane >= 4 * heads) & (lane < 5 * heads), second, mixed)
    return jnp.where(lane < SPLIT * heads, -mixed, 0.0)


def key_times(pieces, heads):
    first, second, third = pieces
    lane = lane_iota((1, LANES))
    mixed = jnp.where(lane < 3 * heads, first, jnp.where(lane < 5 * heads, second, third))
    return jnp.where(lane < SPLIT * heads, mixed, 0.0)


def value_times(pieces, heads):
    first, second, third = pieces
    lane = lane_iota((1, LANES))
    place = jnp.where(lane >= HEAD, lane - HEAD, lane)
    pairs = heads // 2
    mixed = jnp.where(place < pairs, first, jnp.where(place < 2 * pairs, second, third))
    return jnp.where(place < 3 * pairs, mixed, 0.0)


def store_rows(ref, pitch, cols, first, value, lane):
    for r in range(value.shape[0] // cols):
        row = value[r * cols : (r + 1) * cols]
        lanes = slice(lane, lane + value.shape[1])
        base = (first + r) * pitch
        ref[base : base + cols, lanes] = row
        ref[base + cols : base + pitch, lanes] = row[: pitch - cols]


def store_key_times(keys, heads, cols, pitch, first, ref, invalid):
    width = heads * HEAD
    times = key_times(time_pieces(keys, heads, lane_heads(heads)), heads)
    place = row_iota((pitch, LANES))
    outside = (place < RAD) | (place >= cols + RAD)
    if invalid is not None:
        outside = outside | invalid
    flag = lane_iota((pitch, LANES)) == SPLIT * heads + BLOCK + RAD
    bias = jnp.where(flag & outside, -BIG, 0.0)
    for r in range(keys.shape[0] // cols):
        row = times[r * cols : (r + 1) * cols]
        row = jnp.concatenate([row, row[: pitch - cols]], axis=0)
        base = (first + r) * pitch
        ref[base : base + pitch, width : width + LANES] = (row + bias).astype(BF16)


def store_value_times(values, heads, cols, pitch, first, ref):
    width = heads * HEAD
    pieces = time_pieces(values, heads, value_lane_heads(heads), heads // 4)
    times = value_times(pieces, heads).astype(BF16)
    store_rows(ref, pitch, cols, first, times, 2 * width + LANES)


def project_strips(strips, k_w, v_w, heads, cols, pitch, ref, invalid):
    width = heads * HEAD
    behind = None
    first = 0
    for weight in (k_w, v_w):
        for number, strip in enumerate(strips):
            first = sum(s.shape[0] for s in strips[:number]) // cols
            points = jnp.dot(strip, weight[...], preferred_element_type=F32).astype(BF16)
            lane = 0 if weight is k_w else width + LANES
            store_rows(ref, pitch, cols, first, points, lane)
            if behind is not None:
                behind()
            if weight is k_w:
                behind = functools.partial(
                    store_key_times, points, heads, cols, pitch, first, ref, invalid
                )
            else:
                behind = functools.partial(
                    store_value_times, points, heads, cols, pitch, first, ref
                )
    behind()


def window_bias(mask_ref, first, heads):
    shape = mask_ref.shape
    place, lane = row_iota(shape), lane_iota(shape)
    key_row = place // WIDE
    key_col = place - key_row * WIDE
    key_row = key_row + first
    col = lane - SPLIT * heads
    row = col - BLOCK
    bad_col = (col >= 0) & (col < BLOCK) & ((key_col < col) | (key_col > col + 2 * RAD))
    bad_row = (row >= 0) & (row < RAD) & ((key_row < row) | (key_row > row + 2 * RAD))
    mask_ref[...] = jnp.where(bad_col | bad_row, -BIG, 0.0).astype(BF16)


def query_features(cols, heads, row):
    shape = (cols, LANES)
    token, lane = row_iota(shape), lane_iota(shape)
    col = lane - SPLIT * heads
    hit = (col == token % BLOCK) | (col == BLOCK + row) | (col == BLOCK + RAD)
    return jnp.where(hit & (col >= 0), 1.0, 0.0)


def head_mask(heads, head, lane, pieces):
    hit = lane == head
    for piece in range(1, pieces):
        hit = hit | (lane == piece * heads + head)
    return hit


def head_scales(scale_ref, heads):
    scale = scale_ref[...][None, :] * DOUBLE_LOG2E
    return [scale[:, h : h + 1] for h in range(heads)]


def as_factor(hit):
    return jnp.where(hit, 1.0, 0.0).astype(BF16)


def window_attention(q_ref, kv_refs, mask_ref, scale_ref, heads, blocks, finish):
    width = heads * HEAD
    extra = width + LANES
    cols = LANES
    rows = q_ref.shape[0] // cols
    pairs = range(heads // 2)
    lane = lane_iota((1, LANES))
    low = lane < HEAD
    sides = [as_factor(low), as_factor(lane >= HEAD)]
    keeps = [
        as_factor(head_mask(heads, h, lane, SPLIT) | (lane >= SPLIT * heads)) for h in range(heads)
    ]
    scale = head_scales(scale_ref, heads)
    half = rows * BLOCK
    parts = (slice(0, half), slice(half, 2 * half))

    def queries_of(block, lanes):
        starts = [r * cols + block * BLOCK for r in range(rows)]
        return jnp.concatenate([q_ref[s : s + BLOCK, lanes] for s in starts], axis=0)

    def keys_of(block, lanes):
        tiles = []
        for ref in kv_refs:
            pitch = ref.shape[0] // rows
            starts = [r * pitch + block * BLOCK for r in range(rows)]
            tiles += [ref[s : s + WIDE, lanes] for s in starts]
        return jnp.concatenate(tiles, axis=0)

    def extras(block):
        return (
            queries_of(block, slice(width, extra)),
            keys_of(block, slice(width, extra)) + mask_ref[...],
        )

    def scores_of(block, pair, qx, kx):
        tile = slice(pair * LANES, (pair + 1) * LANES)
        q = queries_of(block, tile)
        stacked = [
            jnp.concatenate([q * sides[i], qx * keeps[2 * pair + i]], axis=1) for i in range(2)
        ]
        return lax.dot_general(
            jnp.concatenate(stacked, axis=0),
            jnp.concatenate([keys_of(block, tile), kx], axis=1),
            NT,
            preferred_element_type=F32,
        )

    first, last = blocks[0], blocks[-1]
    extra_now = extras(first)
    scores = [scores_of(first, pair, *extra_now) for pair in pairs]
    behind = None
    for block in blocks:
        ahead = extras(block + 1) if block < last else None
        peaks, coming = [], []
        for pair in pairs:
            peaks.append(jnp.max(scores[pair], axis=-1, keepdims=True))
            if ahead is not None:
                coming.append(scores_of(block + 1, pair, *ahead))
        vx = keys_of(block, slice(extra + width, 2 * extra))
        totals = []
        for pair in pairs:
            both = [
                jnp.exp2((scores[pair][part] - peaks[pair][part]) * scale[2 * pair + i])
                for i, part in enumerate(parts)
            ]
            weights = jnp.concatenate(both, axis=0).astype(BF16)
            v = keys_of(block, slice(extra + pair * LANES, extra + (pair + 1) * LANES))
            totals.append(
                jnp.dot(weights, jnp.concatenate([v, vx], axis=1), preferred_element_type=F32)
            )
            if behind is not None:
                finish(block - 1, pair, *behind[pair])
        behind = []
        for pair in pairs:
            total, peak = totals[pair], peaks[pair]
            behind.append(
                (
                    jnp.where(low, peak[parts[0]], peak[parts[1]]),
                    jnp.where(low, total[parts[0], :LANES], total[parts[1], :LANES]),
                    jnp.where(low, total[parts[0], LANES:], total[parts[1], LANES:]),
                    jnp.where(low, scale[2 * pair], scale[2 * pair + 1]),
                )
            )
        scores = coming
    for pair in pairs:
        finish(last, pair, *behind[pair])


def setup_body(near_mask, far_mask, *, heads):
    half = near_mask.shape[0] // 2
    odd = lax.axis_index(AXIS) % 2
    window_bias(near_mask.at[:half], RAD, heads)
    window_bias(near_mask.at[half:], 2 * RAD * (1 - odd), heads)
    window_bias(far_mask, 2 * RAD * odd, heads)


def project_body(mask_ref, gain_ref, own_ref, k_w, v_w, kv_ref, normed_ref):
    del mask_ref
    cells, width = own_ref.shape
    heads = width // HEAD
    cols = LANES
    rows = cells // cols
    pitch = kv_ref.shape[0] // rows
    gain = gain_ref[...][None, :]
    shifted = []
    for r in range(rows):
        part = slice(r * cols, (r + 1) * cols)
        normed = normalize(own_ref[part], gain)
        normed_ref[part] = normed.astype(BF16)
        shifted.append(pltpu.roll(normed, RAD, 0).astype(BF16))
    halves = [jnp.concatenate(shifted[i : i + 2], axis=0) for i in range(0, rows, 2)]
    project_strips(halves, k_w, v_w, heads, cols, pitch, kv_ref, None)


def query_body(scale_ref, pool_ref, normed_ref, q_w, kv_ref, q_ref, out_ref):
    pq = pool_ref[...]
    count, width = pq.shape
    heads = width // HEAD
    cols = LANES
    extra = width + LANES
    rows = normed_ref.shape[0] // cols
    pitch = kv_ref.shape[0] // rows
    lane = lane_iota((count, LANES))
    q_time = query_times(time_pieces(pq, heads, lane_heads(heads)), heads)
    zero = jnp.zeros((count, LANES), F32)
    q_rows = []
    for h in range(heads):
        tiles = [zero] * (width // LANES)
        tile = pq[:, h // 2 * LANES : (h // 2 + 1) * LANES].astype(F32)
        tiles[h // 2] = jnp.where((lane < HEAD) if h % 2 == 0 else (lane >= HEAD), tile, 0.0)
        tiles.append(jnp.where(head_mask(heads, h, lane, SPLIT), q_time, 0.0))
        q_rows.append(jnp.concatenate(tiles, axis=1))
    q_all = jnp.concatenate(q_rows, axis=0).astype(BF16)
    keys = jnp.concatenate(
        [kv_ref[r * pitch : r * pitch + cols, :extra] for r in range(rows)], axis=0
    )
    queries = jnp.dot(normed_ref[...], q_w[...], preferred_element_type=F32).astype(BF16)
    q_ref[:, :width] = queries
    scores = lax.dot_general(q_all, keys, NT, preferred_element_type=F32)
    times = query_times(time_pieces(queries, heads, lane_heads(heads)), heads)
    for r in range(rows):
        part = slice(r * cols, (r + 1) * cols)
        q_ref[part, width:] = (times[part] + query_features(cols, heads, r)).astype(BF16)
    scale = jnp.concatenate(
        [jnp.broadcast_to(c, (count, 1)) for c in head_scales(scale_ref, heads)], axis=0
    )
    scores = scores * scale
    peak = jnp.max(scores, axis=-1, keepdims=True)
    f = jnp.exp2(scores - peak)
    hi = f.astype(BF16)
    lo = (f - hi.astype(F32)).astype(BF16)
    values = jnp.concatenate(
        [kv_ref[r * pitch : r * pitch + cols, extra:] for r in range(rows)], axis=0
    )
    total = jnp.dot(jnp.concatenate([hi, lo], axis=0), values, preferred_element_type=F32)
    total = total[: heads * count] + total[heads * count :]
    stats = jnp.zeros((count, LANES), F32)
    for h in range(heads):
        part = slice(h * count, (h + 1) * count)
        time = jnp.where(value_mask(heads, h), total[part, width:], 0.0)
        stats = jnp.where(lane == h, jnp.sum(time, axis=-1, keepdims=True), stats)
        stats = jnp.where(lane == HEAD + h, peak[part], stats)
    for j in range(width // LANES):
        tile = slice(j * LANES, (j + 1) * LANES)
        first = total[2 * j * count : (2 * j + 1) * count, tile]
        second = total[(2 * j + 1) * count : (2 * j + 2) * count, tile]
        out_ref[j * count : (j + 1) * count, :] = jnp.where(lane < HEAD, first, second)
    out_ref[width // LANES * count :, :] = stats


def near_body(scale_ref, q_ref, own_ref, mate_ref, mask_ref, peak_ref, space_ref, time_ref, *, blocks):
    width = q_ref.shape[1] - LANES
    heads = width // HEAD
    size = q_ref.shape[0] // LANES * BLOCK
    mine = [value_mask(heads, 2 * j) | value_mask(heads, 2 * j + 1) for j in range(heads // 2)]
    block_times = {}

    def finish(block, pair, peak, space, times, scale):
        place = block - blocks[0]
        part = slice(place * size, (place + 1) * size)
        tile = slice(pair * LANES, (pair + 1) * LANES)
        peak_ref[part, tile] = peak
        space_ref[part, tile] = space
        so_far = block_times.get(block)
        times = times if so_far is None else jnp.where(mine[pair], times, so_far)
        block_times[block] = times
        if pair == heads // 2 - 1:
            time_ref[part, :] = times

    window_attention(q_ref, (own_ref, mate_ref), mask_ref, scale_ref, heads, blocks, finish)


def far_keys_body(gain_ref, far_ref, k_w, v_w, kv_ref):
    cells, width = far_ref.shape
    heads = width // HEAD
    cols = LANES
    rows = cells // cols
    pitch = kv_ref.shape[0] // rows
    index = lax.axis_index(AXIS)
    invalid = (index == 0) | (index == lax.axis_size(AXIS) - 1)
    gain = gain_ref[...][None, :]
    shifted = []
    for r in range(rows):
        normed = normalize(far_ref[r * cols : (r + 1) * cols], gain)
        shifted.append(pltpu.roll(normed, RAD, 0).astype(BF16))
    halves = [jnp.concatenate(shifted[i : i + 2], axis=0) for i in range(0, rows, 2)]
    project_strips(halves, k_w, v_w, heads, cols, pitch, kv_ref, invalid)


def far_first_body(*refs, blocks):
    *inputs, out_hbm, mix_ref, out_ref, sems = refs
    far_blocks(*inputs, out_hbm, mix_ref, out_ref, sems, blocks)


def far_last_body(so_far, part_ref, other_ref, *refs, blocks, count, step):
    del so_far
    *inputs, out_hbm, pooled_hbm, mix_ref, out_ref, sems, pooled_ref, pooled_sem = refs
    merge_body(part_ref, other_ref, pooled_ref, count=count, step=step, last=True)
    copy = pltpu.make_async_copy(pooled_ref, pooled_hbm, pooled_sem)
    copy.start()
    far_blocks(*inputs, out_hbm, mix_ref, out_ref, sems, blocks)
    copy.wait()


def far_blocks(
    scale_ref, kv_ref, o_w, own_ref, q_ref, mask_ref, peak_ref, space_ref, time_ref,
    out_hbm, mix_ref, out_ref, sems, blocks,
):
    width = own_ref.shape[1]
    heads = width // HEAD
    cols = LANES
    rows = own_ref.shape[0] // cols
    size = rows * BLOCK
    strip = 2 * BLOCK
    chunk0 = blocks[0] // 2
    low = lane_iota((1, LANES)) < HEAD
    mine = [value_mask(heads, 2 * j) | value_mask(heads, 2 * j + 1) for j in range(heads // 2)]

    def copy_out(chunk):
        columns = slice(chunk * strip, (chunk + 1) * strip)
        place = chunk - chunk0
        return pltpu.make_async_copy(out_ref.at[place], out_hbm.at[:, columns], sems.at[place])

    def mix_out(chunk):
        projected = jnp.dot(mix_ref[chunk - chunk0], o_w[...], preferred_element_type=F32)
        for r in range(rows):
            start = r * cols + chunk * strip
            tokens = own_ref[start : start + strip].astype(F32)
            mixed = tokens + projected[r * strip : (r + 1) * strip]
            out_ref[chunk - chunk0, r] = mixed.astype(BF16)
        copy_out(chunk).start()

    def finish(block, pair, far_peak, far_space, far_times, scale):
        place = (block - blocks[0]) * size
        part = slice(place, place + size)
        tile = slice(pair * LANES, (pair + 1) * LANES)
        near_peak = peak_ref[part, tile]
        peak = jnp.maximum(near_peak, far_peak)
        near = jnp.exp2((near_peak - peak) * scale)
        far = jnp.exp2((far_peak - peak) * scale)
        mean = space_ref[part, tile] * near + far_space * far
        times = jnp.where(mine[pair], time_ref[part, :] * near + far_times * far, 0.0)
        time = jnp.where(low, *half_sums(times))
        spread = time * time - jnp.where(low, *half_sums(mean * mean))
        attended = (mean * lax.rsqrt(spread)).astype(BF16)
        chunk, side = block // 2, block % 2
        for r in range(rows):
            start = (2 * r + side) * BLOCK
            mix_ref[chunk - chunk0, start : start + BLOCK, tile] = attended[r * BLOCK : (r + 1) * BLOCK]
        if side and pair == heads // 2 - 1:
            mix_out(chunk)

    window_attention(q_ref, (kv_ref,), mask_ref, scale_ref, heads, blocks, finish)
    for chunk in range(chunk0, chunk0 + len(blocks) // 2):
        copy_out(chunk).wait()


def merge_body(mine_ref, other_ref, out_ref, *, count, step, last):
    upper = (lax.axis_index(AXIS) // step) % 2 > 0
    mine, other = mine_ref[...], other_ref[...]
    first, second = jnp.where(upper, other, mine), jnp.where(upper, mine, other)
    lane = lane_iota((count, LANES))
    low = lane < HEAD
    tiles = first.shape[0] // count - 1
    s1, s2 = first[tiles * count :], second[tiles * count :]
    peak = jnp.maximum(s1, s2)
    f1 = jnp.exp2(jnp.where(low, 0.0, s1 - peak))
    f2 = jnp.exp2(jnp.where(low, 0.0, s2 - peak))
    time = s1 * pltpu.roll(f1, HEAD, 1) + s2 * pltpu.roll(f2, HEAD, 1)
    stats = jnp.where(low, time, peak)
    for j in range(tiles):
        part = slice(j * count, (j + 1) * count)
        a, b = HEAD + 2 * j, HEAD + 2 * j + 1
        g1 = jnp.where(low, f1[:, a : a + 1], f1[:, b : b + 1])
        g2 = jnp.where(low, f2[:, a : a + 1], f2[:, b : b + 1])
        mean = first[part] * g1 + second[part] * g2
        if not last:
            out_ref[part, :] = mean
            continue
        time = jnp.where(low, stats[:, 2 * j : 2 * j + 1], stats[:, 2 * j + 1 : 2 * j + 2])
        one, two = half_sums(mean * mean)
        out_ref[:, j * LANES : (j + 1) * LANES] = mean / jnp.sqrt(
            time * time - jnp.where(low, one, two)
        )
    if not last:
        out_ref[tiles * count :, :] = stats


VMEM = pl.BlockSpec(memory_space=pltpu.VMEM)
HBM = pl.BlockSpec(memory_space=pltpu.HBM)


def local_call(
    body, specs, args, outs, scratch=(), limit=24, flops=None, out_specs=None, aliases=None
):
    return pl.pallas_call(
        body,
        out_shape=outs,
        in_specs=list(specs),
        out_specs=out_specs or jax.tree.map(lambda _: VMEM, outs),
        scratch_shapes=list(scratch),
        input_output_aliases=aliases or {},
        cost_estimate=flops
        and pl.CostEstimate(flops=flops, transcendentals=0, bytes_accessed=0),
        compiler_params=pltpu.CompilerParams(vmem_limit_bytes=limit << 20),
    )(*args)


def hop_steps(ring):
    return [1] + [1 << bit for bit in range(2, ring.bit_length() - 1)] + [2]


def exchange(value, pairs):
    return lax.ppermute(value, AXIS, pairs)


def per_device(
    tokens, norm_gain, query_weight, key_weight, value_weight, out_weight, head_scale, pool_queries
):
    rows, cols, width = tokens.shape
    heads = head_scale.shape[0]
    count = pool_queries.shape[0]
    ring = lax.axis_size(AXIS)
    assert rows == RAD and cols == LANES and width == heads * HEAD
    assert ring & (ring - 1) == 0 and ring > 8
    struct = jax.ShapeDtypeStruct
    cells = rows * cols
    own = tokens.reshape(cells, width)
    swap = [(i, i ^ 1) for i in range(ring)]
    cross = [(i, i + 1) for i in range(1, ring - 1, 2)]
    cross = cross + [(b, a) for a, b in cross]
    far = exchange(own, cross)
    extra = width + LANES
    pitch = cols + WIDE - BLOCK
    near_mask, far_mask = local_call(
        functools.partial(setup_body, heads=heads),
        (),
        (),
        (struct((2 * rows * WIDE, LANES), BF16), struct((rows * WIDE, LANES), BF16)),
        limit=8,
        flops=1 << 32,
    )
    keys_values, normed = local_call(
        project_body,
        (VMEM,) * 5,
        (near_mask, norm_gain, own, key_weight, value_weight),
        (struct((rows * pitch, 2 * extra), BF16), struct((cells, width), BF16)),
    )
    mate = exchange(keys_values, swap)
    queries, part = local_call(
        query_body,
        (VMEM,) * 5,
        (head_scale, pool_queries, normed, query_weight, keys_values),
        (
            struct((cells, extra), BF16),
            struct(((width // LANES + 1) * count, LANES), F32),
        ),
    )
    near = []
    split = cols // BLOCK // 2
    for blocks in (range(split), range(split, 2 * split)):
        size = split * rows * BLOCK
        near.append(local_call(
            lambda *refs, blocks=blocks: near_body(*refs, blocks=blocks),
            (VMEM,) * 5,
            (head_scale, queries, keys_values, mate, near_mask),
            (
                struct((size, width), F32),
                struct((size, width), F32),
                struct((size, LANES), F32),
            ),
        ))
    steps = hop_steps(ring)
    for step in steps:
        other = exchange(part, [(i, i ^ step) for i in range(ring)])
        if step == steps[-1]:
            break
        part = local_call(
            lambda *refs, step=step: merge_body(*refs, count=count, step=step, last=False),
            (VMEM, VMEM),
            (part, other),
            struct(part.shape, F32),
            limit=4,
        )
    far_keys_values = local_call(
        far_keys_body,
        (VMEM,) * 4,
        (norm_gain, far, key_weight, value_weight),
        struct((rows * pitch, 2 * extra), BF16),
    )
    shared = (head_scale, far_keys_values, out_weight, own, queries, far_mask)
    chunks = split // 2
    scratch = [
        pltpu.VMEM((chunks, 2 * rows * BLOCK, width), BF16),
        pltpu.VMEM((chunks, rows, 2 * BLOCK, width), BF16),
        pltpu.SemaphoreType.DMA((chunks,)),
    ]
    mixed = local_call(
        functools.partial(far_first_body, blocks=range(split)),
        (VMEM,) * 9,
        shared + tuple(near[0]),
        struct(tokens.shape, BF16),
        scratch,
        out_specs=HBM,
    )
    return local_call(
        functools.partial(
            far_last_body, blocks=range(split, 2 * split), count=count, step=steps[-1]
        ),
        (HBM,) + (VMEM,) * 11,
        (mixed, part, other) + shared + tuple(near[1]),
        (struct(tokens.shape, BF16), struct((count, width), F32)),
        scratch + [pltpu.VMEM((count, width), F32), pltpu.SemaphoreType.DMA(())],
        out_specs=(HBM, HBM),
        aliases={0: 0},
    )


def solution(mesh):
    placed = (P(("slide", "row"), None, None), P(), P(), P(), P(), P(), P(), P())
    return jax.shard_map(
        per_device,
        mesh=mesh,
        in_specs=placed,
        out_specs=(P(("slide", "row"), None, None), P("slide", None)),
        check_vma=False,
    )
```

```python
import functools
import math

import jax
import jax.numpy as jnp
from jax import lax
from jax.experimental import pallas as pl
from jax.experimental.pallas import tpu as pltpu
from jax.sharding import PartitionSpec as P


RAD = 4
EPS = 1e-06
HEAD = 64
LANES = 128
BLOCK = 16
WIDE = 2 * BLOCK
NEAR_LAGS = (10, 5, 5)
FAR_LAGS = (4, 2, 2)
SPLIT = 6
BIG = 1e30
F32 = jnp.float32
BF16 = jnp.bfloat16
DOUBLE_LOG2E = 2.0 * math.log2(math.e)
NT = (((1,), (1,)), ((), ()))
AXIS = "row"


def lane_iota(shape):
    return lax.broadcasted_iota(jnp.int32, shape, len(shape) - 1)


def row_iota(shape):
    return lax.broadcasted_iota(jnp.int32, shape, 0)


def normalize(tokens, gain):
    feats = tokens.astype(F32)
    mean_sq = jnp.mean(feats * feats, axis=-1, keepdims=True)
    return feats * lax.rsqrt(mean_sq + EPS) * gain


def lane_heads(heads):
    lane = lane_iota((1, LANES))
    head = lane
    for piece in range(1, LANES // heads + 1):
        head = jnp.where(lane >= piece * heads, lane - piece * heads, head)
    return head


def value_lane_heads(heads):
    lane = lane_iota((1, LANES))
    high = jnp.where(lane >= HEAD, 1, 0)
    place = lane - HEAD * high
    pairs = heads // 2
    rest = place
    for piece in range(1, 3):
        rest = jnp.where(place >= piece * pairs, place - piece * pairs, rest)
    return jnp.where(place < 3 * pairs, 2 * rest + high, -1)


def value_mask(heads, head):
    lane = lane_iota((1, LANES))
    first = HEAD * (head % 2) + head // 2
    pairs = heads // 2
    return (lane == first) | (lane == first + pairs) | (lane == first + 2 * pairs)


def half_sums(squares):
    low = lane_iota((1, LANES)) < HEAD
    return (
        jnp.sum(jnp.where(low, squares, 0.0), axis=-1, keepdims=True),
        jnp.sum(jnp.where(low, 0.0, squares), axis=-1, keepdims=True),
    )


def time_pieces(points, heads, head, matmul_tiles=0):
    tiles = heads // 2
    split = (tiles - matmul_tiles) * LANES
    total = jnp.zeros((points.shape[0], LANES), F32)
    if matmul_tiles:
        f = points[:, split:].astype(F32)
        sq = f * f
        hi = sq.astype(BF16)
        lo = (sq - hi.astype(F32)).astype(BF16)
        hit = row_iota((sq.shape[1], LANES)) // HEAD + split // HEAD == head
        sums = as_factor(hit)
        total = jnp.dot(hi, sums, preferred_element_type=F32)
        total = total + jnp.dot(lo, sums, preferred_element_type=F32)
    for j in range(tiles - matmul_tiles):
        f = points[:, j * LANES : (j + 1) * LANES].astype(F32)
        first, second = half_sums(f * f)
        total = jnp.where(head == 2 * j, first, jnp.where(head == 2 * j + 1, second, total))
    total = 1.0 + total
    t = total * lax.rsqrt(total)
    first = t.astype(BF16).astype(F32)
    rest = t - first
    second = rest.astype(BF16).astype(F32)
    third = (rest - second).astype(BF16).astype(F32)
    return first, second, third


def query_times(pieces, heads):
    first, second, third = pieces
    lane = lane_iota((1, LANES))
    mixed = jnp.where((lane >= heads) & (lane < 2 * heads), second, first)
    mixed = jnp.where((lane >= 2 * heads) & (lane < 3 * heads), third, mixed)
    mixed = jnp.where((lane >= 4 * heads) & (lane < 5 * heads), second, mixed)
    return jnp.where(lane < SPLIT * heads, -mixed, 0.0)


def key_times(pieces, heads):
    first, second, third = pieces
    lane = lane_iota((1, LANES))
    mixed = jnp.where(lane < 3 * heads, first, jnp.where(lane < 5 * heads, second, third))
    return jnp.where(lane < SPLIT * heads, mixed, 0.0)


def value_times(pieces, heads):
    first, second, third = pieces
    lane = lane_iota((1, LANES))
    place = jnp.where(lane >= HEAD, lane - HEAD, lane)
    pairs = heads // 2
    mixed = jnp.where(place < pairs, first, jnp.where(place < 2 * pairs, second, third))
    return jnp.where(place < 3 * pairs, mixed, 0.0)


def store_rows(ref, pitch, cols, first, value, lane):
    for r in range(value.shape[0] // cols):
        row = value[r * cols : (r + 1) * cols]
        lanes = slice(lane, lane + value.shape[1])
        base = (first + r) * pitch
        ref[base : base + cols, lanes] = row
        ref[base + cols : base + pitch, lanes] = row[: pitch - cols]


def store_key_times(keys, heads, cols, pitch, first, ref, invalid):
    width = heads * HEAD
    times = key_times(time_pieces(keys, heads, lane_heads(heads)), heads)
    place = row_iota((pitch, LANES))
    outside = (place < RAD) | (place >= cols + RAD)
    if invalid is not None:
        outside = outside | invalid
    flag = lane_iota((pitch, LANES)) == SPLIT * heads + BLOCK + RAD
    bias = jnp.where(flag & outside, -BIG, 0.0)
    for r in range(keys.shape[0] // cols):
        row = times[r * cols : (r + 1) * cols]
        row = jnp.concatenate([row, row[: pitch - cols]], axis=0)
        base = (first + r) * pitch
        ref[base : base + pitch, width : width + LANES] = (row + bias).astype(BF16)


def store_value_times(values, heads, cols, pitch, first, ref):
    width = heads * HEAD
    pieces = time_pieces(values, heads, value_lane_heads(heads), heads // 3)
    times = value_times(pieces, heads).astype(BF16)
    store_rows(ref, pitch, cols, first, times, 2 * width + LANES)


def project_strips(strips, k_w, v_w, heads, cols, pitch, ref, invalid):
    width = heads * HEAD
    made, waiting = [], None
    for weight in (k_w, v_w):
        first = 0
        for number, strip in enumerate(strips):
            if number == len(made):
                made.append(strip())
            points = jnp.dot(made[number], weight[...], preferred_element_type=F32).astype(BF16)
            store_rows(ref, pitch, cols, first, points, 0 if weight is k_w else width + LANES)
            if waiting is not None:
                waiting()
            if weight is k_w:
                waiting = functools.partial(
                    store_key_times, points, heads, cols, pitch, first, ref, invalid
                )
            else:
                waiting = functools.partial(
                    store_value_times, points, heads, cols, pitch, first, ref
                )
            first += points.shape[0] // cols
    waiting()


def shifted_strips(token_ref, gain, cols, normed_ref=None):
    def strip(start):
        rows = []
        for begin in (start, start + cols):
            part = slice(begin, begin + cols)
            normed = normalize(token_ref[part], gain)
            if normed_ref is not None:
                normed_ref[part] = normed.astype(BF16)
            rows.append(pltpu.roll(normed, RAD, 0).astype(BF16))
        return jnp.concatenate(rows, axis=0)

    return [functools.partial(strip, i) for i in range(0, token_ref.shape[0], 2 * cols)]


def window_bias(mask_ref, first, heads):
    shape = mask_ref.shape
    place, lane = row_iota(shape), lane_iota(shape)
    key_row = place // WIDE
    key_col = place - key_row * WIDE
    key_row = key_row + first
    col = lane - SPLIT * heads
    row = col - BLOCK
    bad_col = (col >= 0) & (col < BLOCK) & ((key_col < col) | (key_col > col + 2 * RAD))
    bad_row = (row >= 0) & (row < RAD) & ((key_row < row) | (key_row > row + 2 * RAD))
    mask_ref[...] = jnp.where(bad_col | bad_row, -BIG, 0.0).astype(BF16)


def query_features(cols, heads, row):
    shape = (cols, LANES)
    token, lane = row_iota(shape), lane_iota(shape)
    col = lane - SPLIT * heads
    hit = (col == token % BLOCK) | (col == BLOCK + row) | (col == BLOCK + RAD)
    return jnp.where(hit & (col >= 0), 1.0, 0.0)


def head_mask(heads, head, lane, pieces):
    hit = lane == head
    for piece in range(1, pieces):
        hit = hit | (lane == piece * heads + head)
    return hit


def head_scales(scale_ref, heads):
    scale = scale_ref[...][None, :] * DOUBLE_LOG2E
    return [scale[:, h : h + 1] for h in range(heads)]


def as_factor(hit):
    return jnp.where(hit, 1.0, 0.0).astype(BF16)


def window_attention(
    q_ref, kv_refs, mask_ref, scale_ref, heads, blocks, lags, finish, beside=()
):
    width = heads * HEAD
    extra = width + LANES
    cols = LANES
    rows = q_ref.shape[0] // cols
    pairs = range(heads // 2)
    lane = lane_iota((1, LANES))
    low = lane < HEAD
    sides = [as_factor(low), as_factor(lane >= HEAD)]
    keeps = [
        as_factor(head_mask(heads, h, lane, SPLIT) | (lane >= SPLIT * heads)) for h in range(heads)
    ]
    scale = head_scales(scale_ref, heads)
    half = rows * BLOCK
    parts = (slice(0, half), slice(half, 2 * half))

    def queries_of(block, lanes):
        starts = [r * cols + block * BLOCK for r in range(rows)]
        return jnp.concatenate([q_ref[s : s + BLOCK, lanes] for s in starts], axis=0)

    def keys_of(block, lanes):
        tiles = []
        for ref in kv_refs:
            pitch = ref.shape[0] // rows
            starts = [r * pitch + block * BLOCK for r in range(rows)]
            tiles += [ref[s : s + WIDE, lanes] for s in starts]
        return jnp.concatenate(tiles, axis=0)

    def extras(block):
        return (
            queries_of(block, slice(width, extra)),
            keys_of(block, slice(width, extra)) + mask_ref[...],
        )

    def scores_of(block, pair, qx, kx):
        tile = slice(pair * LANES, (pair + 1) * LANES)
        q = queries_of(block, tile)
        stacked = [
            jnp.concatenate([q * sides[i], qx * keeps[2 * pair + i]], axis=1) for i in range(2)
        ]
        return lax.dot_general(
            jnp.concatenate(stacked, axis=0),
            jnp.concatenate([keys_of(block, tile), kx], axis=1),
            NT,
            preferred_element_type=F32,
        )

    steps = [(block, pair) for block in blocks for pair in pairs]
    block_extras, scores, peaks, results = {}, {}, {}, {}

    def score(step):
        block, pair = steps[step]
        if block not in block_extras:
            block_extras[block] = extras(block)
        scores[step] = scores_of(block, pair, *block_extras[block])

    def find_peak(step):
        peaks[step] = jnp.max(scores[step], axis=-1, keepdims=True)

    def attend(step):
        block, pair = steps[step]
        now, peak = scores.pop(step), peaks.pop(step)
        both = [
            jnp.exp2((now[part] - peak[part]) * scale[2 * pair + i])
            for i, part in enumerate(parts)
        ]
        weights = jnp.concatenate(both, axis=0).astype(BF16)
        v = keys_of(block, slice(extra + pair * LANES, extra + (pair + 1) * LANES))
        vx = keys_of(block, slice(extra + width, 2 * extra))
        total = jnp.dot(weights, jnp.concatenate([v, vx], axis=1), preferred_element_type=F32)
        results[step] = (
            jnp.where(low, peak[parts[0]], peak[parts[1]]),
            jnp.where(low, total[parts[0], :LANES], total[parts[1], :LANES]),
            jnp.where(low, total[parts[0], LANES:], total[parts[1], LANES:]),
            jnp.where(low, scale[2 * pair], scale[2 * pair + 1]),
        )

    count = len(steps)
    beside = list(beside)
    ahead, early, behind = lags
    for step in range(-ahead, count + behind):
        if step + ahead < count:
            score(step + ahead)
        if 0 <= step + early < count:
            find_peak(step + early)
        if 0 <= step < count:
            attend(step)
        if beside and step >= 0:
            beside.pop(0)()
        if step - behind >= 0:
            finish(*steps[step - behind], *results.pop(step - behind))


def setup_body(near_mask, far_mask, *, heads):
    half = near_mask.shape[0] // 2
    odd = lax.axis_index(AXIS) % 2
    window_bias(near_mask.at[:half], RAD, heads)
    window_bias(near_mask.at[half:], 2 * RAD * (1 - odd), heads)
    window_bias(far_mask, 2 * RAD * odd, heads)


def project_body(mask_ref, gain_ref, own_ref, k_w, v_w, kv_ref, normed_ref):
    del mask_ref
    cells, width = own_ref.shape
    heads = width // HEAD
    cols = LANES
    rows = cells // cols
    pitch = kv_ref.shape[0] // rows
    strips = shifted_strips(own_ref, gain_ref[...][None, :], cols, normed_ref)
    project_strips(strips, k_w, v_w, heads, cols, pitch, kv_ref, None)


def query_body(scale_ref, pool_ref, normed_ref, q_w, kv_ref, q_ref, out_ref):
    pq = pool_ref[...]
    count, width = pq.shape
    heads = width // HEAD
    cols = LANES
    extra = width + LANES
    rows = normed_ref.shape[0] // cols
    pitch = kv_ref.shape[0] // rows
    lane = lane_iota((count, LANES))
    q_time = query_times(time_pieces(pq, heads, lane_heads(heads)), heads)
    zero = jnp.zeros((count, LANES), F32)
    q_rows = []
    for h in range(heads):
        tiles = [zero] * (width // LANES)
        tile = pq[:, h // 2 * LANES : (h // 2 + 1) * LANES].astype(F32)
        tiles[h // 2] = jnp.where((lane < HEAD) if h % 2 == 0 else (lane >= HEAD), tile, 0.0)
        tiles.append(jnp.where(head_mask(heads, h, lane, SPLIT), q_time, 0.0))
        q_rows.append(jnp.concatenate(tiles, axis=1))
    q_all = jnp.concatenate(q_rows, axis=0).astype(BF16)
    keys = jnp.concatenate(
        [kv_ref[r * pitch : r * pitch + cols, :extra] for r in range(rows)], axis=0
    )
    queries = jnp.dot(normed_ref[...], q_w[...], preferred_element_type=F32).astype(BF16)
    q_ref[:, :width] = queries
    scores = lax.dot_general(q_all, keys, NT, preferred_element_type=F32)
    times = query_times(time_pieces(queries, heads, lane_heads(heads)), heads)
    for r in range(rows):
        part = slice(r * cols, (r + 1) * cols)
        q_ref[part, width:] = (times[part] + query_features(cols, heads, r)).astype(BF16)
    scale = jnp.concatenate(
        [jnp.broadcast_to(c, (count, 1)) for c in head_scales(scale_ref, heads)], axis=0
    )
    scores = scores * scale
    peak = jnp.max(scores, axis=-1, keepdims=True)
    f = jnp.exp2(scores - peak)
    hi = f.astype(BF16)
    lo = (f - hi.astype(F32)).astype(BF16)
    values = jnp.concatenate(
        [kv_ref[r * pitch : r * pitch + cols, extra:] for r in range(rows)], axis=0
    )
    total = jnp.dot(jnp.concatenate([hi, lo], axis=0), values, preferred_element_type=F32)
    total = total[: heads * count] + total[heads * count :]
    stats = jnp.zeros((count, LANES), F32)
    for h in range(heads):
        part = slice(h * count, (h + 1) * count)
        time = jnp.where(value_mask(heads, h), total[part, width:], 0.0)
        stats = jnp.where(lane == h, jnp.sum(time, axis=-1, keepdims=True), stats)
        stats = jnp.where(lane == HEAD + h, peak[part], stats)
    for j in range(width // LANES):
        tile = slice(j * LANES, (j + 1) * LANES)
        first = total[2 * j * count : (2 * j + 1) * count, tile]
        second = total[(2 * j + 1) * count : (2 * j + 2) * count, tile]
        out_ref[j * count : (j + 1) * count, :] = jnp.where(lane < HEAD, first, second)
    out_ref[width // LANES * count :, :] = stats


def near_body(scale_ref, q_ref, own_ref, mate_ref, mask_ref, peak_ref, space_ref, time_ref, *, blocks):
    width = q_ref.shape[1] - LANES
    heads = width // HEAD
    size = q_ref.shape[0] // LANES * BLOCK
    mine = [value_mask(heads, 2 * j) | value_mask(heads, 2 * j + 1) for j in range(heads // 2)]
    block_times = {}

    def finish(block, pair, peak, space, times, scale):
        place = block - blocks[0]
        part = slice(place * size, (place + 1) * size)
        tile = slice(pair * LANES, (pair + 1) * LANES)
        peak_ref[part, tile] = peak
        space_ref[part, tile] = space
        so_far = block_times.get(block)
        times = times if so_far is None else jnp.where(mine[pair], times, so_far)
        block_times[block] = times
        if pair == heads // 2 - 1:
            time_ref[part, :] = times

    window_attention(
        q_ref, (own_ref, mate_ref), mask_ref, scale_ref, heads, blocks, NEAR_LAGS, finish
    )


def far_first_body(
    gain_ref, far_ref, k_w, v_w, scale_ref, q_ref, mask_ref, peak_ref, space_ref, time_ref,
    kv_ref, mix_ref, *, blocks,
):
    cells, width = far_ref.shape
    heads = width // HEAD
    cols = LANES
    rows = cells // cols
    pitch = kv_ref.shape[0] // rows
    index = lax.axis_index(AXIS)
    invalid = (index == 0) | (index == lax.axis_size(AXIS) - 1)
    strips = shifted_strips(far_ref, gain_ref[...][None, :], cols)
    project_strips(strips, k_w, v_w, heads, cols, pitch, kv_ref, invalid)
    near = (peak_ref, space_ref, time_ref)
    far_blocks(scale_ref, kv_ref, q_ref, mask_ref, near, mix_ref, blocks)


def far_last_body(
    part_ref, other_ref, o_w, own_ref, first_ref,
    scale_ref, kv_ref, q_ref, mask_ref, peak_ref, space_ref, time_ref,
    out_hbm, pooled_hbm, mix_ref, out_ref, pooled_ref, sems, *, blocks, count, step,
):
    cols = LANES
    rows = own_ref.shape[0] // cols
    strip = 2 * BLOCK
    chunks = cols // strip
    chunk0 = blocks[0] // 2

    def copy_out(chunk):
        columns = slice(chunk * strip, (chunk + 1) * strip)
        return pltpu.make_async_copy(out_ref.at[chunk], out_hbm.at[:, columns], sems.at[chunk])

    def mix_out(chunk):
        attended = first_ref[chunk] if chunk < chunk0 else mix_ref[chunk - chunk0]
        projected = jnp.dot(attended, o_w[...], preferred_element_type=F32)
        for r in range(rows):
            start = r * cols + chunk * strip
            tokens = own_ref[start : start + strip].astype(F32)
            mixed = tokens + projected[r * strip : (r + 1) * strip]
            out_ref[chunk, r] = mixed.astype(BF16)
        copy_out(chunk).start()

    pooled_copy = pltpu.make_async_copy(pooled_ref, pooled_hbm, sems.at[chunks])

    def pool():
        merge_body(part_ref, other_ref, pooled_ref, count=count, step=step, last=True)
        pooled_copy.start()

    near = (peak_ref, space_ref, time_ref)
    beside = [functools.partial(mix_out, chunk) for chunk in range(chunk0)] + [pool]
    far_blocks(scale_ref, kv_ref, q_ref, mask_ref, near, mix_ref, blocks, mix_out, beside)
    for chunk in range(chunks):
        copy_out(chunk).wait()
    pooled_copy.wait()


def far_blocks(
    scale_ref, kv_ref, q_ref, mask_ref, near_refs, mix_ref, blocks, chunk_done=None, beside=()
):
    peak_ref, space_ref, time_ref = near_refs
    width = q_ref.shape[1] - LANES
    heads = width // HEAD
    rows = q_ref.shape[0] // LANES
    size = rows * BLOCK
    chunk0 = blocks[0] // 2
    low = lane_iota((1, LANES)) < HEAD
    mine = [value_mask(heads, 2 * j) | value_mask(heads, 2 * j + 1) for j in range(heads // 2)]

    def finish(block, pair, far_peak, far_space, far_times, scale):
        place = (block - blocks[0]) * size
        part = slice(place, place + size)
        tile = slice(pair * LANES, (pair + 1) * LANES)
        near_peak = peak_ref[part, tile]
        peak = jnp.maximum(near_peak, far_peak)
        near = jnp.exp2((near_peak - peak) * scale)
        far = jnp.exp2((far_peak - peak) * scale)
        mean = space_ref[part, tile] * near + far_space * far
        times = jnp.where(mine[pair], time_ref[part, :] * near + far_times * far, 0.0)
        time = jnp.where(low, *half_sums(times))
        spread = time * time - jnp.where(low, *half_sums(mean * mean))
        attended = (mean * lax.rsqrt(spread)).astype(BF16)
        chunk, side = block // 2, block % 2
        for r in range(rows):
            start = (2 * r + side) * BLOCK
            mix_ref[chunk - chunk0, start : start + BLOCK, tile] = attended[
                r * BLOCK : (r + 1) * BLOCK
            ]
        if chunk_done is not None and side and pair == heads // 2 - 1:
            chunk_done(chunk)

    window_attention(
        q_ref, (kv_ref,), mask_ref, scale_ref, heads, blocks, FAR_LAGS, finish, beside
    )


def merge_body(mine_ref, other_ref, out_ref, *, count, step, last):
    upper = (lax.axis_index(AXIS) // step) % 2 > 0
    mine, other = mine_ref[...], other_ref[...]
    first, second = jnp.where(upper, other, mine), jnp.where(upper, mine, other)
    lane = lane_iota((count, LANES))
    low = lane < HEAD
    tiles = first.shape[0] // count - 1
    s1, s2 = first[tiles * count :], second[tiles * count :]
    peak = jnp.maximum(s1, s2)
    f1 = jnp.exp2(jnp.where(low, 0.0, s1 - peak))
    f2 = jnp.exp2(jnp.where(low, 0.0, s2 - peak))
    time = s1 * pltpu.roll(f1, HEAD, 1) + s2 * pltpu.roll(f2, HEAD, 1)
    stats = jnp.where(low, time, peak)
    for j in range(tiles):
        part = slice(j * count, (j + 1) * count)
        a, b = HEAD + 2 * j, HEAD + 2 * j + 1
        g1 = jnp.where(low, f1[:, a : a + 1], f1[:, b : b + 1])
        g2 = jnp.where(low, f2[:, a : a + 1], f2[:, b : b + 1])
        mean = first[part] * g1 + second[part] * g2
        if not last:
            out_ref[part, :] = mean
            continue
        time = jnp.where(low, stats[:, 2 * j : 2 * j + 1], stats[:, 2 * j + 1 : 2 * j + 2])
        one, two = half_sums(mean * mean)
        out_ref[:, j * LANES : (j + 1) * LANES] = mean / jnp.sqrt(
            time * time - jnp.where(low, one, two)
        )
    if not last:
        out_ref[tiles * count :, :] = stats


VMEM = pl.BlockSpec(memory_space=pltpu.VMEM)
HBM = pl.BlockSpec(memory_space=pltpu.HBM)


def local_call(body, specs, args, outs, scratch=(), limit=24, flops=None, out_specs=None):
    return pl.pallas_call(
        body,
        out_shape=outs,
        in_specs=list(specs),
        out_specs=out_specs or jax.tree.map(lambda _: VMEM, outs),
        scratch_shapes=list(scratch),
        cost_estimate=flops
        and pl.CostEstimate(flops=flops, transcendentals=0, bytes_accessed=0),
        compiler_params=pltpu.CompilerParams(vmem_limit_bytes=limit << 20),
    )(*args)


def hop_steps(ring):
    return [1] + [1 << bit for bit in range(2, ring.bit_length() - 1)] + [2]


def exchange(value, pairs):
    return lax.ppermute(value, AXIS, pairs)


def per_device(
    tokens, norm_gain, query_weight, key_weight, value_weight, out_weight, head_scale, pool_queries
):
    rows, cols, width = tokens.shape
    heads = head_scale.shape[0]
    count = pool_queries.shape[0]
    ring = lax.axis_size(AXIS)
    assert rows == RAD and cols == LANES and width == heads * HEAD
    assert ring & (ring - 1) == 0 and ring > 8
    struct = jax.ShapeDtypeStruct
    cells = rows * cols
    own = tokens.reshape(cells, width)
    swap = [(i, i ^ 1) for i in range(ring)]
    cross = [(i, i + 1) for i in range(1, ring - 1, 2)]
    cross = cross + [(b, a) for a, b in cross]
    far = exchange(own, cross)
    extra = width + LANES
    pitch = cols + WIDE - BLOCK
    near_mask, far_mask = local_call(
        functools.partial(setup_body, heads=heads),
        (),
        (),
        (struct((2 * rows * WIDE, LANES), BF16), struct((rows * WIDE, LANES), BF16)),
        limit=8,
        flops=1 << 32,
    )
    keys_values, normed = local_call(
        project_body,
        (VMEM,) * 5,
        (near_mask, norm_gain, own, key_weight, value_weight),
        (struct((rows * pitch, 2 * extra), BF16), struct((cells, width), BF16)),
    )
    mate = exchange(keys_values, swap)
    queries, part = local_call(
        query_body,
        (VMEM,) * 5,
        (head_scale, pool_queries, normed, query_weight, keys_values),
        (
            struct((cells, extra), BF16),
            struct(((width // LANES + 1) * count, LANES), F32),
        ),
    )
    near = []
    split = cols // BLOCK // 2
    for blocks in (range(split), range(split, 2 * split)):
        size = split * rows * BLOCK
        near.append(local_call(
            lambda *refs, blocks=blocks: near_body(*refs, blocks=blocks),
            (VMEM,) * 5,
            (head_scale, queries, keys_values, mate, near_mask),
            (
                struct((size, width), F32),
                struct((size, width), F32),
                struct((size, LANES), F32),
            ),
        ))
    steps = hop_steps(ring)
    for step in steps:
        other = exchange(part, [(i, i ^ step) for i in range(ring)])
        if step == steps[-1]:
            break
        part = local_call(
            lambda *refs, step=step: merge_body(*refs, count=count, step=step, last=False),
            (VMEM, VMEM),
            (part, other),
            struct(part.shape, F32),
            limit=4,
        )
    chunks = split // 2
    mix = struct((chunks, 2 * rows * BLOCK, width), BF16)
    far_keys_values, first_mix = local_call(
        functools.partial(far_first_body, blocks=range(split)),
        (VMEM,) * 10,
        (norm_gain, far, key_weight, value_weight, head_scale, queries, far_mask, *near[0]),
        (struct((rows * pitch, 2 * extra), BF16), mix),
    )
    return local_call(
        functools.partial(
            far_last_body, blocks=range(split, 2 * split), count=count, step=steps[-1]
        ),
        (VMEM,) * 12,
        (part, other, out_weight, own, first_mix, head_scale, far_keys_values, queries, far_mask)
        + tuple(near[1]),
        (struct(tokens.shape, BF16), struct((count, width), F32)),
        [
            pltpu.VMEM(mix.shape, BF16),
            pltpu.VMEM((2 * chunks, rows, 2 * BLOCK, width), BF16),
            pltpu.VMEM((count, width), F32),
            pltpu.SemaphoreType.DMA((2 * chunks + 1,)),
        ],
        out_specs=(HBM, HBM),
    )


def solution(mesh):
    placed = (P(("slide", "row"), None, None), P(), P(), P(), P(), P(), P(), P())
    return jax.shard_map(
        per_device,
        mesh=mesh,
        in_specs=placed,
        out_specs=(P(("slide", "row"), None, None), P("slide", None)),
        check_vma=False,
    )
```

```python
import functools
import math

import jax
import jax.numpy as jnp
from jax import lax
from jax.experimental import pallas as pl
from jax.experimental.pallas import tpu as pltpu
from jax.sharding import PartitionSpec as P


RAD = 4
EPS = 1e-06
HEAD = 64
LANES = 128
BLOCK = 16
WIDE = 2 * BLOCK
SPLIT = 6
BIG = 1e30
F32 = jnp.float32
BF16 = jnp.bfloat16
DOUBLE_LOG2E = 2.0 * math.log2(math.e)
NT = (((1,), (1,)), ((), ()))
AXIS = "row"


def lane_iota(shape):
    return lax.broadcasted_iota(jnp.int32, shape, len(shape) - 1)


def row_iota(shape):
    return lax.broadcasted_iota(jnp.int32, shape, 0)


def normalize(tokens, gain):
    feats = tokens.astype(F32)
    mean_sq = jnp.mean(feats * feats, axis=-1, keepdims=True)
    return feats * lax.rsqrt(mean_sq + EPS) * gain


def lane_heads(heads):
    lane = lane_iota((1, LANES))
    head = lane
    for piece in range(1, LANES // heads + 1):
        head = jnp.where(lane >= piece * heads, lane - piece * heads, head)
    return head


def value_lane_heads(heads):
    lane = lane_iota((1, LANES))
    high = jnp.where(lane >= HEAD, 1, 0)
    place = lane - HEAD * high
    pairs = heads // 2
    rest = place
    for piece in range(1, 3):
        rest = jnp.where(place >= piece * pairs, place - piece * pairs, rest)
    return jnp.where(place < 3 * pairs, 2 * rest + high, -1)


def value_mask(heads, head):
    lane = lane_iota((1, LANES))
    first = HEAD * (head % 2) + head // 2
    pairs = heads // 2
    return (lane == first) | (lane == first + pairs) | (lane == first + 2 * pairs)


def half_sums(squares):
    low = lane_iota((1, LANES)) < HEAD
    return (
        jnp.sum(jnp.where(low, squares, 0.0), axis=-1, keepdims=True),
        jnp.sum(jnp.where(low, 0.0, squares), axis=-1, keepdims=True),
    )


def time_pieces(points, heads, head, matmul_tiles=0):
    tiles = heads // 2
    split = (tiles - matmul_tiles) * LANES
    total = jnp.zeros((points.shape[0], LANES), F32)
    if matmul_tiles:
        f = points[:, split:].astype(F32)
        sq = f * f
        hi = sq.astype(BF16)
        lo = (sq - hi.astype(F32)).astype(BF16)
        hit = row_iota((sq.shape[1], LANES)) // HEAD + split // HEAD == head
        sums = as_factor(hit)
        total = jnp.dot(hi, sums, preferred_element_type=F32)
        total = total + jnp.dot(lo, sums, preferred_element_type=F32)
    for j in range(tiles - matmul_tiles):
        f = points[:, j * LANES : (j + 1) * LANES].astype(F32)
        first, second = half_sums(f * f)
        total = jnp.where(head == 2 * j, first, jnp.where(head == 2 * j + 1, second, total))
    total = 1.0 + total
    t = total * lax.rsqrt(total)
    first = t.astype(BF16).astype(F32)
    rest = t - first
    second = rest.astype(BF16).astype(F32)
    third = (rest - second).astype(BF16).astype(F32)
    return first, second, third


def query_times(pieces, heads):
    first, second, third = pieces
    lane = lane_iota((1, LANES))
    mixed = jnp.where((lane >= heads) & (lane < 2 * heads), second, first)
    mixed = jnp.where((lane >= 2 * heads) & (lane < 3 * heads), third, mixed)
    mixed = jnp.where((lane >= 4 * heads) & (lane < 5 * heads), second, mixed)
    return jnp.where(lane < SPLIT * heads, -mixed, 0.0)


def key_times(pieces, heads):
    first, second, third = pieces
    lane = lane_iota((1, LANES))
    mixed = jnp.where(lane < 3 * heads, first, jnp.where(lane < 5 * heads, second, third))
    return jnp.where(lane < SPLIT * heads, mixed, 0.0)


def value_times(pieces, heads):
    first, second, third = pieces
    lane = lane_iota((1, LANES))
    place = jnp.where(lane >= HEAD, lane - HEAD, lane)
    pairs = heads // 2
    mixed = jnp.where(place < pairs, first, jnp.where(place < 2 * pairs, second, third))
    return jnp.where(place < 3 * pairs, mixed, 0.0)


def store_rows(ref, pitch, cols, first, value, lane):
    for r in range(value.shape[0] // cols):
        row = value[r * cols : (r + 1) * cols]
        lanes = slice(lane, lane + value.shape[1])
        base = (first + r) * pitch
        ref[base : base + cols, lanes] = row
        ref[base + cols : base + pitch, lanes] = row[: pitch - cols]


def store_key_times(keys, heads, cols, pitch, first, ref, invalid):
    width = heads * HEAD
    times = key_times(time_pieces(keys, heads, lane_heads(heads)), heads)
    place = row_iota((pitch, LANES))
    outside = (place < RAD) | (place >= cols + RAD)
    if invalid is not None:
        outside = outside | invalid
    flag = lane_iota((pitch, LANES)) == SPLIT * heads + BLOCK + RAD
    bias = jnp.where(flag & outside, -BIG, 0.0)
    for r in range(keys.shape[0] // cols):
        row = times[r * cols : (r + 1) * cols]
        row = jnp.concatenate([row, row[: pitch - cols]], axis=0)
        base = (first + r) * pitch
        ref[base : base + pitch, width : width + LANES] = (row + bias).astype(BF16)


def store_value_times(values, heads, cols, pitch, first, ref):
    width = heads * HEAD
    pieces = time_pieces(values, heads, value_lane_heads(heads), heads // 3)
    times = value_times(pieces, heads).astype(BF16)
    store_rows(ref, pitch, cols, first, times, 2 * width + LANES)


def project_strips(strips, k_w, v_w, heads, cols, pitch, ref, invalid):
    width = heads * HEAD
    behind = None
    first = 0
    for weight in (k_w, v_w):
        for number, strip in enumerate(strips):
            first = sum(s.shape[0] for s in strips[:number]) // cols
            points = jnp.dot(strip, weight[...], preferred_element_type=F32).astype(BF16)
            lane = 0 if weight is k_w else width + LANES
            store_rows(ref, pitch, cols, first, points, lane)
            if behind is not None:
                behind()
            if weight is k_w:
                behind = functools.partial(
                    store_key_times, points, heads, cols, pitch, first, ref, invalid
                )
            else:
                behind = functools.partial(
                    store_value_times, points, heads, cols, pitch, first, ref
                )
    behind()


def window_bias(mask_ref, first, heads):
    shape = mask_ref.shape
    place, lane = row_iota(shape), lane_iota(shape)
    key_row = place // WIDE
    key_col = place - key_row * WIDE
    key_row = key_row + first
    col = lane - SPLIT * heads
    row = col - BLOCK
    bad_col = (col >= 0) & (col < BLOCK) & ((key_col < col) | (key_col > col + 2 * RAD))
    bad_row = (row >= 0) & (row < RAD) & ((key_row < row) | (key_row > row + 2 * RAD))
    mask_ref[...] = jnp.where(bad_col | bad_row, -BIG, 0.0).astype(BF16)


def query_features(cols, heads, row):
    shape = (cols, LANES)
    token, lane = row_iota(shape), lane_iota(shape)
    col = lane - SPLIT * heads
    hit = (col == token % BLOCK) | (col == BLOCK + row) | (col == BLOCK + RAD)
    return jnp.where(hit & (col >= 0), 1.0, 0.0)


def head_mask(heads, head, lane, pieces):
    hit = lane == head
    for piece in range(1, pieces):
        hit = hit | (lane == piece * heads + head)
    return hit


def head_scales(scale_ref, heads):
    scale = scale_ref[...][None, :] * DOUBLE_LOG2E
    return [scale[:, h : h + 1] for h in range(heads)]


def as_factor(hit):
    return jnp.where(hit, 1.0, 0.0).astype(BF16)


def window_attention(q_ref, kv_refs, mask_ref, scale_ref, heads, blocks, finish):
    width = heads * HEAD
    extra = width + LANES
    cols = LANES
    rows = q_ref.shape[0] // cols
    pairs = range(heads // 2)
    lane = lane_iota((1, LANES))
    low = lane < HEAD
    sides = [as_factor(low), as_factor(lane >= HEAD)]
    keeps = [
        as_factor(head_mask(heads, h, lane, SPLIT) | (lane >= SPLIT * heads)) for h in range(heads)
    ]
    scale = head_scales(scale_ref, heads)
    half = rows * BLOCK
    parts = (slice(0, half), slice(half, 2 * half))

    def queries_of(block, lanes):
        starts = [r * cols + block * BLOCK for r in range(rows)]
        return jnp.concatenate([q_ref[s : s + BLOCK, lanes] for s in starts], axis=0)

    def keys_of(block, lanes):
        tiles = []
        for ref in kv_refs:
            pitch = ref.shape[0] // rows
            starts = [r * pitch + block * BLOCK for r in range(rows)]
            tiles += [ref[s : s + WIDE, lanes] for s in starts]
        return jnp.concatenate(tiles, axis=0)

    def extras(block):
        return (
            queries_of(block, slice(width, extra)),
            keys_of(block, slice(width, extra)) + mask_ref[...],
        )

    def scores_of(block, pair, qx, kx):
        tile = slice(pair * LANES, (pair + 1) * LANES)
        q = queries_of(block, tile)
        stacked = [
            jnp.concatenate([q * sides[i], qx * keeps[2 * pair + i]], axis=1) for i in range(2)
        ]
        return lax.dot_general(
            jnp.concatenate(stacked, axis=0),
            jnp.concatenate([keys_of(block, tile), kx], axis=1),
            NT,
            preferred_element_type=F32,
        )

    first, last = blocks[0], blocks[-1]
    extra_now = extras(first)
    scores = [scores_of(first, pair, *extra_now) for pair in pairs]
    behind = None
    for block in blocks:
        ahead = extras(block + 1) if block < last else None
        peaks, coming = [], []
        for pair in pairs:
            peaks.append(jnp.max(scores[pair], axis=-1, keepdims=True))
            if ahead is not None:
                coming.append(scores_of(block + 1, pair, *ahead))
        vx = keys_of(block, slice(extra + width, 2 * extra))
        totals = []
        for pair in pairs:
            both = [
                jnp.exp2((scores[pair][part] - peaks[pair][part]) * scale[2 * pair + i])
                for i, part in enumerate(parts)
            ]
            weights = jnp.concatenate(both, axis=0).astype(BF16)
            v = keys_of(block, slice(extra + pair * LANES, extra + (pair + 1) * LANES))
            totals.append(
                jnp.dot(weights, jnp.concatenate([v, vx], axis=1), preferred_element_type=F32)
            )
            if behind is not None:
                finish(block - 1, pair, *behind[pair])
        behind = []
        for pair in pairs:
            total, peak = totals[pair], peaks[pair]
            behind.append(
                (
                    jnp.where(low, peak[parts[0]], peak[parts[1]]),
                    jnp.where(low, total[parts[0], :LANES], total[parts[1], :LANES]),
                    jnp.where(low, total[parts[0], LANES:], total[parts[1], LANES:]),
                    jnp.where(low, scale[2 * pair], scale[2 * pair + 1]),
                )
            )
        scores = coming
    for pair in pairs:
        finish(last, pair, *behind[pair])


def setup_body(near_mask, far_mask, *, heads):
    half = near_mask.shape[0] // 2
    odd = lax.axis_index(AXIS) % 2
    window_bias(near_mask.at[:half], RAD, heads)
    window_bias(near_mask.at[half:], 2 * RAD * (1 - odd), heads)
    window_bias(far_mask, 2 * RAD * odd, heads)


def project_body(mask_ref, gain_ref, own_ref, k_w, v_w, kv_ref, normed_ref):
    del mask_ref
    cells, width = own_ref.shape
    heads = width // HEAD
    cols = LANES
    rows = cells // cols
    pitch = kv_ref.shape[0] // rows
    gain = gain_ref[...][None, :]
    shifted = []
    for r in range(rows):
        part = slice(r * cols, (r + 1) * cols)
        normed = normalize(own_ref[part], gain)
        normed_ref[part] = normed.astype(BF16)
        shifted.append(pltpu.roll(normed, RAD, 0).astype(BF16))
    halves = [jnp.concatenate(shifted[i : i + 2], axis=0) for i in range(0, rows, 2)]
    project_strips(halves, k_w, v_w, heads, cols, pitch, kv_ref, None)


def query_body(scale_ref, pool_ref, normed_ref, q_w, kv_ref, q_ref, out_ref):
    pq = pool_ref[...]
    count, width = pq.shape
    heads = width // HEAD
    cols = LANES
    extra = width + LANES
    rows = normed_ref.shape[0] // cols
    pitch = kv_ref.shape[0] // rows
    lane = lane_iota((count, LANES))
    q_time = query_times(time_pieces(pq, heads, lane_heads(heads)), heads)
    zero = jnp.zeros((count, LANES), F32)
    q_rows = []
    for h in range(heads):
        tiles = [zero] * (width // LANES)
        tile = pq[:, h // 2 * LANES : (h // 2 + 1) * LANES].astype(F32)
        tiles[h // 2] = jnp.where((lane < HEAD) if h % 2 == 0 else (lane >= HEAD), tile, 0.0)
        tiles.append(jnp.where(head_mask(heads, h, lane, SPLIT), q_time, 0.0))
        q_rows.append(jnp.concatenate(tiles, axis=1))
    q_all = jnp.concatenate(q_rows, axis=0).astype(BF16)
    keys = jnp.concatenate(
        [kv_ref[r * pitch : r * pitch + cols, :extra] for r in range(rows)], axis=0
    )
    queries = jnp.dot(normed_ref[...], q_w[...], preferred_element_type=F32).astype(BF16)
    q_ref[:, :width] = queries
    scores = lax.dot_general(q_all, keys, NT, preferred_element_type=F32)
    times = query_times(time_pieces(queries, heads, lane_heads(heads)), heads)
    for r in range(rows):
        part = slice(r * cols, (r + 1) * cols)
        q_ref[part, width:] = (times[part] + query_features(cols, heads, r)).astype(BF16)
    scale = jnp.concatenate(
        [jnp.broadcast_to(c, (count, 1)) for c in head_scales(scale_ref, heads)], axis=0
    )
    scores = scores * scale
    peak = jnp.max(scores, axis=-1, keepdims=True)
    f = jnp.exp2(scores - peak)
    hi = f.astype(BF16)
    lo = (f - hi.astype(F32)).astype(BF16)
    values = jnp.concatenate(
        [kv_ref[r * pitch : r * pitch + cols, extra:] for r in range(rows)], axis=0
    )
    total = jnp.dot(jnp.concatenate([hi, lo], axis=0), values, preferred_element_type=F32)
    total = total[: heads * count] + total[heads * count :]
    stats = jnp.zeros((count, LANES), F32)
    for h in range(heads):
        part = slice(h * count, (h + 1) * count)
        time = jnp.where(value_mask(heads, h), total[part, width:], 0.0)
        stats = jnp.where(lane == h, jnp.sum(time, axis=-1, keepdims=True), stats)
        stats = jnp.where(lane == HEAD + h, peak[part], stats)
    for j in range(width // LANES):
        tile = slice(j * LANES, (j + 1) * LANES)
        first = total[2 * j * count : (2 * j + 1) * count, tile]
        second = total[(2 * j + 1) * count : (2 * j + 2) * count, tile]
        out_ref[j * count : (j + 1) * count, :] = jnp.where(lane < HEAD, first, second)
    out_ref[width // LANES * count :, :] = stats


def near_body(scale_ref, q_ref, own_ref, mate_ref, mask_ref, peak_ref, space_ref, time_ref, *, blocks):
    width = q_ref.shape[1] - LANES
    heads = width // HEAD
    size = q_ref.shape[0] // LANES * BLOCK
    mine = [value_mask(heads, 2 * j) | value_mask(heads, 2 * j + 1) for j in range(heads // 2)]
    block_times = {}

    def finish(block, pair, peak, space, times, scale):
        place = block - blocks[0]
        part = slice(place * size, (place + 1) * size)
        tile = slice(pair * LANES, (pair + 1) * LANES)
        peak_ref[part, tile] = peak
        space_ref[part, tile] = space
        so_far = block_times.get(block)
        times = times if so_far is None else jnp.where(mine[pair], times, so_far)
        block_times[block] = times
        if pair == heads // 2 - 1:
            time_ref[part, :] = times

    window_attention(q_ref, (own_ref, mate_ref), mask_ref, scale_ref, heads, blocks, finish)


def far_first_body(
    gain_ref, far_ref, k_w, v_w, scale_ref, q_ref, mask_ref, peak_ref, space_ref, time_ref,
    kv_ref, mix_ref, *, blocks,
):
    cells, width = far_ref.shape
    heads = width // HEAD
    cols = LANES
    rows = cells // cols
    pitch = kv_ref.shape[0] // rows
    index = lax.axis_index(AXIS)
    invalid = (index == 0) | (index == lax.axis_size(AXIS) - 1)
    gain = gain_ref[...][None, :]
    shifted = []
    for r in range(rows):
        normed = normalize(far_ref[r * cols : (r + 1) * cols], gain)
        shifted.append(pltpu.roll(normed, RAD, 0).astype(BF16))
    halves = [jnp.concatenate(shifted[i : i + 2], axis=0) for i in range(0, rows, 2)]
    project_strips(halves, k_w, v_w, heads, cols, pitch, kv_ref, invalid)
    near = (peak_ref, space_ref, time_ref)
    far_blocks(scale_ref, kv_ref, q_ref, mask_ref, near, mix_ref, blocks, None)


def far_last_body(
    part_ref, other_ref, o_w, own_ref, first_ref,
    scale_ref, kv_ref, q_ref, mask_ref, peak_ref, space_ref, time_ref,
    out_hbm, pooled_hbm, mix_ref, out_ref, pooled_ref, sems, *, blocks, count, step,
):
    cols = LANES
    rows = own_ref.shape[0] // cols
    strip = 2 * BLOCK
    chunks = cols // strip
    chunk0 = blocks[0] // 2

    def copy_out(chunk):
        columns = slice(chunk * strip, (chunk + 1) * strip)
        return pltpu.make_async_copy(out_ref.at[chunk], out_hbm.at[:, columns], sems.at[chunk])

    def mix_out(chunk):
        attended = first_ref[chunk] if chunk < chunk0 else mix_ref[chunk - chunk0]
        projected = jnp.dot(attended, o_w[...], preferred_element_type=F32)
        for r in range(rows):
            start = r * cols + chunk * strip
            tokens = own_ref[start : start + strip].astype(F32)
            mixed = tokens + projected[r * strip : (r + 1) * strip]
            out_ref[chunk, r] = mixed.astype(BF16)
        copy_out(chunk).start()

    for chunk in range(chunk0):
        mix_out(chunk)
    merge_body(part_ref, other_ref, pooled_ref, count=count, step=step, last=True)
    pooled_copy = pltpu.make_async_copy(pooled_ref, pooled_hbm, sems.at[chunks])
    pooled_copy.start()
    near = (peak_ref, space_ref, time_ref)
    far_blocks(scale_ref, kv_ref, q_ref, mask_ref, near, mix_ref, blocks, mix_out)
    for chunk in range(chunks):
        copy_out(chunk).wait()
    pooled_copy.wait()


def far_blocks(scale_ref, kv_ref, q_ref, mask_ref, near_refs, mix_ref, blocks, chunk_done):
    peak_ref, space_ref, time_ref = near_refs
    width = q_ref.shape[1] - LANES
    heads = width // HEAD
    rows = q_ref.shape[0] // LANES
    size = rows * BLOCK
    chunk0 = blocks[0] // 2
    low = lane_iota((1, LANES)) < HEAD
    mine = [value_mask(heads, 2 * j) | value_mask(heads, 2 * j + 1) for j in range(heads // 2)]

    def finish(block, pair, far_peak, far_space, far_times, scale):
        place = (block - blocks[0]) * size
        part = slice(place, place + size)
        tile = slice(pair * LANES, (pair + 1) * LANES)
        near_peak = peak_ref[part, tile]
        peak = jnp.maximum(near_peak, far_peak)
        near = jnp.exp2((near_peak - peak) * scale)
        far = jnp.exp2((far_peak - peak) * scale)
        mean = space_ref[part, tile] * near + far_space * far
        times = jnp.where(mine[pair], time_ref[part, :] * near + far_times * far, 0.0)
        time = jnp.where(low, *half_sums(times))
        spread = time * time - jnp.where(low, *half_sums(mean * mean))
        attended = (mean * lax.rsqrt(spread)).astype(BF16)
        chunk, side = block // 2, block % 2
        for r in range(rows):
            start = (2 * r + side) * BLOCK
            mix_ref[chunk - chunk0, start : start + BLOCK, tile] = attended[
                r * BLOCK : (r + 1) * BLOCK
            ]
        if chunk_done is not None and side and pair == heads // 2 - 1:
            chunk_done(chunk)

    window_attention(q_ref, (kv_ref,), mask_ref, scale_ref, heads, blocks, finish)


def merge_body(mine_ref, other_ref, out_ref, *, count, step, last):
    upper = (lax.axis_index(AXIS) // step) % 2 > 0
    mine, other = mine_ref[...], other_ref[...]
    first, second = jnp.where(upper, other, mine), jnp.where(upper, mine, other)
    lane = lane_iota((count, LANES))
    low = lane < HEAD
    tiles = first.shape[0] // count - 1
    s1, s2 = first[tiles * count :], second[tiles * count :]
    peak = jnp.maximum(s1, s2)
    f1 = jnp.exp2(jnp.where(low, 0.0, s1 - peak))
    f2 = jnp.exp2(jnp.where(low, 0.0, s2 - peak))
    time = s1 * pltpu.roll(f1, HEAD, 1) + s2 * pltpu.roll(f2, HEAD, 1)
    stats = jnp.where(low, time, peak)
    for j in range(tiles):
        part = slice(j * count, (j + 1) * count)
        a, b = HEAD + 2 * j, HEAD + 2 * j + 1
        g1 = jnp.where(low, f1[:, a : a + 1], f1[:, b : b + 1])
        g2 = jnp.where(low, f2[:, a : a + 1], f2[:, b : b + 1])
        mean = first[part] * g1 + second[part] * g2
        if not last:
            out_ref[part, :] = mean
            continue
        time = jnp.where(low, stats[:, 2 * j : 2 * j + 1], stats[:, 2 * j + 1 : 2 * j + 2])
        one, two = half_sums(mean * mean)
        out_ref[:, j * LANES : (j + 1) * LANES] = mean / jnp.sqrt(
            time * time - jnp.where(low, one, two)
        )
    if not last:
        out_ref[tiles * count :, :] = stats


VMEM = pl.BlockSpec(memory_space=pltpu.VMEM)
HBM = pl.BlockSpec(memory_space=pltpu.HBM)


def local_call(body, specs, args, outs, scratch=(), limit=24, flops=None, out_specs=None):
    return pl.pallas_call(
        body,
        out_shape=outs,
        in_specs=list(specs),
        out_specs=out_specs or jax.tree.map(lambda _: VMEM, outs),
        scratch_shapes=list(scratch),
        cost_estimate=flops
        and pl.CostEstimate(flops=flops, transcendentals=0, bytes_accessed=0),
        compiler_params=pltpu.CompilerParams(vmem_limit_bytes=limit << 20),
    )(*args)


def hop_steps(ring):
    return [1] + [1 << bit for bit in range(2, ring.bit_length() - 1)] + [2]


def exchange(value, pairs):
    return lax.ppermute(value, AXIS, pairs)


def per_device(
    tokens, norm_gain, query_weight, key_weight, value_weight, out_weight, head_scale, pool_queries
):
    rows, cols, width = tokens.shape
    heads = head_scale.shape[0]
    count = pool_queries.shape[0]
    ring = lax.axis_size(AXIS)
    assert rows == RAD and cols == LANES and width == heads * HEAD
    assert ring & (ring - 1) == 0 and ring > 8
    struct = jax.ShapeDtypeStruct
    cells = rows * cols
    own = tokens.reshape(cells, width)
    swap = [(i, i ^ 1) for i in range(ring)]
    cross = [(i, i + 1) for i in range(1, ring - 1, 2)]
    cross = cross + [(b, a) for a, b in cross]
    far = exchange(own, cross)
    extra = width + LANES
    pitch = cols + WIDE - BLOCK
    near_mask, far_mask = local_call(
        functools.partial(setup_body, heads=heads),
        (),
        (),
        (struct((2 * rows * WIDE, LANES), BF16), struct((rows * WIDE, LANES), BF16)),
        limit=8,
        flops=1 << 32,
    )
    keys_values, normed = local_call(
        project_body,
        (VMEM,) * 5,
        (near_mask, norm_gain, own, key_weight, value_weight),
        (struct((rows * pitch, 2 * extra), BF16), struct((cells, width), BF16)),
    )
    mate = exchange(keys_values, swap)
    queries, part = local_call(
        query_body,
        (VMEM,) * 5,
        (head_scale, pool_queries, normed, query_weight, keys_values),
        (
            struct((cells, extra), BF16),
            struct(((width // LANES + 1) * count, LANES), F32),
        ),
    )
    near = []
    split = cols // BLOCK // 2
    for blocks in (range(split), range(split, 2 * split)):
        size = split * rows * BLOCK
        near.append(local_call(
            lambda *refs, blocks=blocks: near_body(*refs, blocks=blocks),
            (VMEM,) * 5,
            (head_scale, queries, keys_values, mate, near_mask),
            (
                struct((size, width), F32),
                struct((size, width), F32),
                struct((size, LANES), F32),
            ),
        ))
    steps = hop_steps(ring)
    for step in steps:
        other = exchange(part, [(i, i ^ step) for i in range(ring)])
        if step == steps[-1]:
            break
        part = local_call(
            lambda *refs, step=step: merge_body(*refs, count=count, step=step, last=False),
            (VMEM, VMEM),
            (part, other),
            struct(part.shape, F32),
            limit=4,
        )
    chunks = split // 2
    mix = struct((chunks, 2 * rows * BLOCK, width), BF16)
    far_keys_values, first_mix = local_call(
        functools.partial(far_first_body, blocks=range(split)),
        (VMEM,) * 10,
        (norm_gain, far, key_weight, value_weight, head_scale, queries, far_mask, *near[0]),
        (struct((rows * pitch, 2 * extra), BF16), mix),
    )
    return local_call(
        functools.partial(
            far_last_body, blocks=range(split, 2 * split), count=count, step=steps[-1]
        ),
        (VMEM,) * 12,
        (part, other, out_weight, own, first_mix, head_scale, far_keys_values, queries, far_mask)
        + tuple(near[1]),
        (struct(tokens.shape, BF16), struct((count, width), F32)),
        [
            pltpu.VMEM(mix.shape, BF16),
            pltpu.VMEM((2 * chunks, rows, 2 * BLOCK, width), BF16),
            pltpu.VMEM((count, width), F32),
            pltpu.SemaphoreType.DMA((2 * chunks + 1,)),
        ],
        out_specs=(HBM, HBM),
    )


def solution(mesh):
    placed = (P(("slide", "row"), None, None), P(), P(), P(), P(), P(), P(), P())
    return jax.shard_map(
        per_device,
        mesh=mesh,
        in_specs=placed,
        out_specs=(P(("slide", "row"), None, None), P("slide", None)),
        check_vma=False,
    )
```
